512 devices in a mesh: gx: 32 (over x_lo, z, core), gy: 16 (over y, x_hi).
Axes of the slice: x: 4 (x_hi: 2, x_lo: 2; x = x_hi * 2 + x_lo), y: 8, z: 8, core: 2. Of those that a mesh axis runs over, the one named last changes fastest.
Arguments:
- currents: bfloat16 [1024, 512, 2, 128], P('gx', 'gy'), may hold values from -6 to 6
- box_count: int32 [1024, 512], P('gx', 'gy'), may hold values from 0 to 128, as said below
- aggregate: bfloat16 [256, 256], replicated, may hold values from -0.375 to 0.375
- near_blocks: bfloat16 [9, 256, 256], replicated, may hold values from -0.125 to 0.125
- low_translator: float32 [16, 2, 128], replicated, may hold values from -1.5 to 1.5
- child_to_parent: bfloat16 [4, 256, 512], replicated, may hold values from -0.1875 to 0.1875
- coarse_list: int32 [512, 256, 16], P('gx', 'gy'), may hold values from 0 to 4095
- coarse_kind: int32 [512, 256, 16], P('gx', 'gy'), may hold values from 0 to 63
- coarse_count: int32 [512, 256], P('gx', 'gy'), may hold values from 1 to 16, as said below
- up_translator: float32 [64, 2, 256], replicated, may hold values from -1.5 to 1.5
- parent_to_child: bfloat16 [4, 512, 256], replicated, may hold values from -0.25 to 0.25
- receive_map: bfloat16 [256, 256], replicated, may hold values from -0.375 to 0.375
Outputs:
- field: float32 [1024, 512, 2, 128], P('gx', 'gy')
The draws below stay inside these ranges and needn't reach their ends.
Inputs may be any that keep to these rules, and one draw needn't show every extreme that they name: `box_count`: ground clutter makes some boxes full and most sparse; some box holds 128 unknowns and some none. `coarse_count`: some list uses all 16 entries.
All inputs are finite; a program needn't handle non-finite values.
Results may differ from the reference program's by a relative error of at most 0.0041.
Values may be sent and summed in bfloat16 or wider, within the bound.
A program may use at most 128 MiB of HBM per device.

```python
import jax
import jax.numpy as jnp
from jax import lax

U = 128
Q = 128
QC = 256
LIST = 16
NOFF = 64
NXB = 1024
NYB = 512
CTX = 16
NCX = 512
NCY = 256
GROUP = 4096


def draw_box_count(key, part):
    first, second = jax.random.split(jax.random.fold_in(key, 11))
    sparse = jax.random.randint(first, (NXB, NYB), 0, U // 4 + 1)
    dense = jax.random.randint(second, (NXB, NYB), 0, 8) == 0
    counts = jnp.where(dense, U, sparse)
    counts = counts.at[0, 0].set(U)
    counts = counts.at[NXB - 1, NYB - 1].set(0)
    return counts.astype(jnp.int32)


def draw_coarse_count(key, part):
    counts = jax.random.randint(jax.random.fold_in(key, 23), (NCX, NCY), 1, LIST + 1)
    counts = counts.at[0, 0].set(LIST)
    counts = counts.at[NCX - 1, NCY - 1].set(1)
    return counts.astype(jnp.int32)


def touch_ends(entries, stream_key, least, top_value):
    shape = entries.shape
    place = [jax.random.randint(jax.random.fold_in(stream_key, axis), (), 0, shape[axis]) for axis in range(len(shape))]
    entries = entries.at[tuple(place)].set(least)
    longest = shape.index(max(shape))
    place[longest] = (place[longest] + 1) % shape[longest]
    return entries.at[tuple(place)].set(top_value)


def steps_of(stream_key, extent, cuts, smallest, high):
    loudness = 1.0
    for position, shards_of in cuts:
        heights = jax.random.uniform(jax.random.fold_in(jax.random.fold_in(stream_key, 6), position), (shards_of,), jnp.float32, smallest / len(cuts), high / len(cuts))
        loudness = loudness * jnp.repeat(jnp.exp(heights), extent[position] // shards_of).reshape((-1,) + (1,) * (len(extent) - 1 - position))
    return loudness


def scatter_about(key, extent, width, bound, cuts=(), kind=jnp.bfloat16):
    drawn = width * jax.random.normal(key, extent, jnp.float32)
    if cuts:
        drawn = drawn * steps_of(key, extent, cuts, -0.22, 0.18)
    return jnp.clip(drawn, -bound, bound).astype(kind)


def setup_inputs(seed: int = 0) -> dict:
    splits = jax.random.split(jax.random.key(seed), 13)
    currents = scatter_about(splits[0], (NXB, NYB, 2, U), 1.0, 6.0, ((0, 32), (1, 16)))
    box_count = draw_box_count(jax.random.fold_in(splits[12], 71), 0)
    aggregate = scatter_about(splits[2], (2 * U, 2 * Q), (2 * U) ** -0.5, 0.375)
    near_blocks = scatter_about(splits[3], (9, 2 * U, 2 * U), (18 * U) ** -0.5, 0.125)
    low_translator = scatter_about(splits[4], (16, 2, Q), 0.25, 1.5, (), jnp.float32)
    child_to_parent = scatter_about(splits[5], (4, 2 * Q, 2 * QC), (8 * Q) ** -0.5, 0.1875)
    coarse_list = touch_ends(jax.random.randint(splits[6], (NCX, NCY, LIST), 0, GROUP), jax.random.fold_in(splits[6], 1), 0, GROUP - 1).astype(jnp.int32)
    coarse_kind = touch_ends(jax.random.randint(splits[7], (NCX, NCY, LIST), 0, NOFF), jax.random.fold_in(splits[7], 1), 0, NOFF - 1).astype(jnp.int32)
    coarse_count = draw_coarse_count(jax.random.fold_in(splits[12], 71), 0)
    up_translator = scatter_about(splits[9], (NOFF, 2, QC), 0.25, 1.5, (), jnp.float32)
    parent_to_child = scatter_about(splits[10], (4, 2 * QC, 2 * Q), (2 * QC) ** -0.5, 0.25)
    receive_map = scatter_about(splits[11], (2 * Q, 2 * U), (2 * Q) ** -0.5, 0.375)
    return dict(currents=currents, box_count=box_count, aggregate=aggregate, near_blocks=near_blocks, low_translator=low_translator, child_to_parent=child_to_parent, coarse_list=coarse_list, coarse_kind=coarse_kind, coarse_count=coarse_count, up_translator=up_translator, parent_to_child=parent_to_child, receive_map=receive_map)


def complex_mul(table, pattern):
    real_part = pattern[..., 0, :].astype(jnp.float32)
    imag_part = pattern[..., 1, :].astype(jnp.float32)
    first = table[..., 0, :] * real_part - table[..., 1, :] * imag_part
    second = table[..., 0, :] * imag_part + table[..., 1, :] * real_part
    return jnp.stack([first, second], axis=-2)


def reference(currents, box_count, aggregate, near_blocks, low_translator, child_to_parent, coarse_list, coarse_kind, coarse_count, up_translator, parent_to_child, receive_map):
    boxes_x, boxes_y = box_count.shape
    mask = jnp.arange(U, dtype=jnp.int32)[None, None, :] < box_count[:, :, None]
    live = jnp.where(mask[:, :, None, :], currents, jnp.zeros_like(currents)).astype(jnp.bfloat16)
    flat_live = live.reshape(boxes_x * boxes_y, 2 * U)
    pattern = jnp.dot(flat_live, aggregate, preferred_element_type=jnp.float32).astype(jnp.bfloat16).reshape(boxes_x, boxes_y, 2, Q)
    padded = jnp.pad(pattern, ((2, 2), (2, 2), (0, 0), (0, 0)))
    lower_in = jnp.zeros((boxes_x, boxes_y, 2, Q), jnp.float32)
    offset = 0
    for shift_x in range(-2, 3):
        for shift_y in range(-2, 3):
            if max(abs(shift_x), abs(shift_y)) < 2:
                continue
            source = padded[2 + shift_x:2 + shift_x + boxes_x, 2 + shift_y:2 + shift_y + boxes_y]
            lower_in = lower_in + complex_mul(low_translator[offset], source)
            offset += 1
    parents_x, parents_y = boxes_x // 2, boxes_y // 2
    children = pattern.reshape(parents_x, 2, parents_y, 2, 2 * Q)
    coarse_sum = jnp.zeros((parents_x * parents_y, 2 * QC), jnp.float32)
    for half_x in range(2):
        for half_y in range(2):
            child = children[:, half_x, :, half_y].reshape(parents_x * parents_y, 2 * Q)
            coarse_sum = coarse_sum + jnp.dot(child, child_to_parent[2 * half_x + half_y], preferred_element_type=jnp.float32)
    coarse = coarse_sum.astype(jnp.bfloat16).reshape(parents_x * parents_y, 2, QC)
    group_base = ((jnp.arange(parents_x, dtype=jnp.int32) // CTX) * GROUP)[:, None]

    def accumulate(slot, total):
        target = group_base + coarse_list[:, :, slot]
        source = coarse[target]
        table = up_translator[coarse_kind[:, :, slot]]
        term = complex_mul(table, source)
        keep = slot < coarse_count
        return total + jnp.where(keep[:, :, None, None], term, jnp.zeros_like(term))

    coarse_acc = lax.fori_loop(0, LIST, accumulate, jnp.zeros((parents_x, parents_y, 2, QC), jnp.float32))
    coarse_in = coarse_acc.astype(jnp.bfloat16).reshape(parents_x * parents_y, 2 * QC)
    pieces = [jnp.dot(coarse_in, parent_to_child[child_id], preferred_element_type=jnp.float32).reshape(parents_x, parents_y, 2 * Q) for child_id in range(4)]
    rows_a = jnp.stack([pieces[0], pieces[1]], axis=2)
    rows_b = jnp.stack([pieces[2], pieces[3]], axis=2)
    from_parent = jnp.stack([rows_a, rows_b], axis=1).reshape(boxes_x, boxes_y, 2 * Q)
    incoming = (lower_in.reshape(boxes_x, boxes_y, 2 * Q) + from_parent).astype(jnp.bfloat16)
    field = jnp.dot(incoming.reshape(boxes_x * boxes_y, 2 * Q), receive_map, preferred_element_type=jnp.float32)
    near_pad = jnp.pad(live, ((1, 1), (1, 1), (0, 0), (0, 0)))
    for shift_x in range(-1, 2):
        for shift_y in range(-1, 2):
            source = near_pad[1 + shift_x:1 + shift_x + boxes_x, 1 + shift_y:1 + shift_y + boxes_y].reshape(boxes_x * boxes_y, 2 * U)
            field = field + jnp.dot(source, near_blocks[3 * (shift_x + 1) + shift_y + 1], preferred_element_type=jnp.float32)
    field = field.reshape(boxes_x, boxes_y, 2, U) * mask[:, :, None, :].astype(jnp.float32)
    return field
```

```python
import functools

import jax
import jax.numpy as jnp
from jax import lax
from jax.experimental import pallas as pl
from jax.experimental.pallas import tpu as pltpu
from jax.sharding import PartitionSpec as P

F32 = jnp.float32
BF16 = jnp.bfloat16
MESH = pl.DeviceIdType.MESH
TX = 32
TY = 32
PITCH = 80
WIDE = TX + 4
ROWS = 1024
FIRST = 448
OFFSETS = [(dx, dy) for dx in range(-2, 3) for dy in range(-2, 3) if max(abs(dx), abs(dy)) == 2]


def remote(src, dst, send, recv, device):
    return pltpu.make_async_remote_copy(
        src_ref=src, dst_ref=dst, send_sem=send, recv_sem=recv, device_id=device, device_id_type=MESH
    )


def gather_kernel(
    n_gx,
    n_gy,
    cur,
    cnt,
    agg,
    near,
    low,
    c2p,
    group,
    lower_out,
    near_out,
    mask_out,
    sel_rows,
    cntb,
    lf,
    pf,
    ll,
    pv,
    cf,
    own,
    s_lo,
    s_hi,
    h_lo,
    h_hi,
    low_v,
    near_v,
    ys,
    yr,
    xs,
    xr,
    hs,
    hr,
    loc,
):
    gx = lax.axis_index("gx")
    gy = lax.axis_index("gy")
    ring = n_gy // 2
    y = gy // 2
    xh = lax.rem(gy, 2)
    px = 1 - xh

    def slot(yy, xx):
        return lax.rem(yy + ring, ring) * 2 + xx

    x_next = {"gx": lax.rem(gx + 1, n_gx)}
    x_prev = {"gx": lax.rem(gx + n_gx - 1, n_gx)}
    y_next = {"gy": lax.rem(gy + 1, n_gy)}
    y_prev = {"gy": lax.rem(gy + n_gy - 1, n_gy)}
    r_next = {"gy": slot(y + 1, xh)}
    r_prev = {"gy": slot(y - 1, xh)}
    r_cross = {"gy": slot(y, px)}
    barrier = pltpu.get_barrier_semaphore()
    for device in (x_next, x_prev, y_next, y_prev, r_next, r_prev):
        pl.semaphore_signal(barrier, inc=1, device_id=device, device_id_type=MESH)

    pick = (
        lax.broadcasted_iota(jnp.int32, (2 * TY, TY), 0) // 2 == lax.broadcasted_iota(jnp.int32, (2 * TY, TY), 1)
    ).astype(F32)
    for i in range(TX):
        line = jnp.broadcast_to(cnt[pl.ds(i, 1), :].astype(F32), (2 * TY, TY))
        sel_rows[pl.ds(2 * TY * i, 2 * TY), :] = (line * pick).astype(BF16)
    cntb[...] = jnp.dot(sel_rows[...], jnp.ones((TY, 128), BF16), preferred_element_type=F32)
    lane = lax.broadcasted_iota(jnp.int32, (2 * TY, 128), 1).astype(F32)
    for i in range(TX):
        rows = pl.ds(2 * TY * i, 2 * TY)
        live = jnp.where(lane < cntb[rows, :], cur[rows, :].astype(F32), 0.0)
        lf[pl.ds(PITCH * (i + 2) + 8, 2 * TY), :] = live

    def piece(ref, x, start):
        real = ref[pl.ds(PITCH * x + start, 16, stride=4), :]
        imag = ref[pl.ds(PITCH * x + start + 1, 16, stride=4), :]
        return real, imag

    def plane(x, k):
        real, imag = piece(lf, x, 6 + 2 * k)
        base = 64 * x + 16 * k
        ll[pl.ds(base, 16), :] = jnp.concatenate([real, imag], axis=1).astype(BF16)

    for i in range(TX):
        for k in (1, 2):
            plane(i + 2, k)

    def lines(ref, x, count, k, planes):
        parts = [ref[pl.ds(64 * (x + n) + 16 * k, 16 * planes), :] for n in range(count)]
        return jnp.concatenate(parts, axis=0)

    def spread(x, b, value):
        for h in range(2):
            pf[pl.ds(PITCH * x + 8 + 2 * b + h, 16, stride=4), :] = value[:, 128 * h : 128 * h + 128]

    for block in range(4):
        got = jnp.dot(lines(ll, 2 + 8 * block, 8, 1, 2), agg[...], preferred_element_type=F32).astype(BF16)
        pv[pl.ds(256 * block, 256), :] = got

    total = jnp.zeros((256, 512), F32)
    for q in range(4):
        child = jnp.concatenate([pv[pl.ds(64 * p + 16 * q, 16), :] for p in range(16)], axis=0)
        total = total + jnp.dot(child, c2p[pl.ds(256 * q, 256), :], preferred_element_type=F32)
    for q in range(4):
        cf[pl.ds(q, 256, stride=4), :] = total[:, 128 * q : 128 * q + 128]
    own[...] = cf[...].astype(BF16)

    pl.semaphore_wait(barrier, 6)

    sign = (1, -1)
    along = (r_next, r_prev)
    sent = []

    def go(copy):
        copy.start()
        sent.append(copy)

    def span(dr, d, w):
        n = ROWS if w == 0 else FIRST
        if d < 3:
            return 0, n
        return (0, n // 2) if dr == 0 else (n // 2, n - n // 2)

    def y_send(dr, d, w):
        start, n = span(dr, d, w)
        where = group.at[slot(y - sign[dr] * d, xh if w == 0 else px), pl.ds(start, n)]
        src = own.at[pl.ds(start, n)] if (d == 0 and w == 0) else where
        go(remote(src, where, ys.at[dr, d, w], yr.at[dr, d, w], along[dr]))

    def y_wait(dr, d, w):
        start, n = span(dr, d, w)
        where = group.at[slot(y - sign[dr] * (d + 1), xh if w == 0 else px), pl.ds(start, n)]
        remote(where, where, ys.at[dr, d, w], yr.at[dr, d, w], along[dr]).wait_recv()

    def x_send(k, yy, start, n, mine=False):
        where = group.at[slot(yy, xh), pl.ds(start, n)]
        src = own.at[pl.ds(start, n)] if mine else where
        go(remote(src, where, xs.at[k], xr.at[k], r_cross))

    def x_wait(k, yy, start, n):
        where = group.at[slot(yy, px), pl.ds(start, n)]
        remote(where, where, xs.at[k], xr.at[k], r_cross).wait_recv()

    x_send(0, y, 0, FIRST, True)
    y_send(0, 0, 0)
    y_send(1, 0, 0)
    x_send(1, y, FIRST, ROWS - FIRST, True)
    local = pltpu.make_async_copy(own, group.at[gy], loc.at[0])
    local.start()

    def x_halo(k):
        src = (2, 3, TX, TX + 1)[k]
        dst = (TX + 2, TX + 3, 0, 1)[k]
        return remote(
            lf.at[pl.ds(PITCH * src + 8, 2 * TY)],
            lf.at[pl.ds(PITCH * dst + 8, 2 * TY)],
            hs.at[k],
            hr.at[k],
            x_prev if k < 2 else x_next,
        )

    halo = [x_halo(k) for k in range(4)]
    for copy in halo:
        copy.start()

    own_lane = lax.broadcasted_iota(jnp.int32, (16, 128), 1).astype(F32)
    for i in range(TX):
        for b in range(2):
            held = cntb[pl.ds(64 * i + 2 * b, 16, stride=4), :]
            mask_out_rows = jnp.where(own_lane < held, 1.0, 0.0)
            cf_rows = pl.ds(32 * i + 16 * b, 16)
            low_v[cf_rows, pl.ds(0, 128)] = mask_out_rows
    mask_copy = pltpu.make_async_copy(low_v.at[:, pl.ds(0, 128)], mask_out, loc.at[1])
    mask_copy.start()
    for i in range(TX):
        for b in range(2):
            spread(i + 2, b, pv[pl.ds(32 * i + 16 * b, 16), :].astype(F32))

    for copy in halo:
        copy.wait()

    @pl.when(gx == 0)
    def _():
        for x in (0, 1):
            lf[pl.ds(PITCH * x + 8, 2 * TY), :] = jnp.zeros((2 * TY, 128), F32)

    @pl.when(gx == n_gx - 1)
    def _():
        for x in (TX + 2, TX + 3):
            lf[pl.ds(PITCH * x + 8, 2 * TY), :] = jnp.zeros((2 * TY, 128), F32)

    for x in range(0, WIDE, 2):
        for buf, start in ((s_lo, 8), (s_hi, 2 * TY)):
            pair = [lf[pl.ds(PITCH * (x + e) + start, 8), :] for e in range(2)]
            buf[pl.ds(8 * x, 16), :] = jnp.concatenate(pair, axis=0).astype(BF16)
    halo_y = [
        remote(s_lo, h_hi, hs.at[4], hr.at[4], y_prev),
        remote(s_hi, h_lo, hs.at[5], hr.at[5], y_next),
    ]
    for copy in halo_y:
        copy.start()

    x_wait(0, y, 0, FIRST)
    y_send(0, 0, 1)
    y_send(1, 0, 1)

    for x in (0, 1, TX + 2, TX + 3):
        for k in (1, 2):
            plane(x, k)
    for x in (0, TX + 2):
        got = jnp.dot(lines(ll, x, 2, 1, 2), agg[...], preferred_element_type=F32).astype(BF16).astype(F32)
        for e in range(2):
            for b in range(2):
                spread(x + e, b, got[32 * e + 16 * b : 32 * e + 16 * b + 16])

    for copy in halo_y:
        copy.wait()

    @pl.when(gy == 0)
    def _():
        h_lo[...] = jnp.zeros_like(h_lo)

    @pl.when(gy == n_gy - 1)
    def _():
        h_hi[...] = jnp.zeros_like(h_hi)

    for x in range(0, WIDE, 2):
        for buf, start in ((h_lo, 0), (h_hi, 2 * TY + 8)):
            pair = buf[pl.ds(8 * x, 16), :].astype(F32)
            for e in range(2):
                lf[pl.ds(PITCH * (x + e) + start, 8), :] = pair[8 * e : 8 * e + 8]

    for start in (4, 6, 2 * TY + 8, 2 * TY + 10):
        cols = [lf[pl.ds(start + h, WIDE, stride=PITCH), :] for h in range(2)]
        lhs = jnp.concatenate(cols, axis=1)
        lhs = jnp.concatenate([lhs, jnp.zeros((48 - WIDE, 256), F32)], axis=0).astype(BF16)
        got = jnp.dot(lhs, agg[...], preferred_element_type=F32).astype(BF16).astype(F32)
        for h in range(2):
            pf[pl.ds(start + h, WIDE, stride=PITCH), :] = got[:WIDE, 128 * h : 128 * h + 128]

    crossed = []

    def step(d, w, dr):
        y_wait(dr, d - 1, w)
        y_send(dr, d, w)
        if w == 0:
            k = 2 + (d - 1) * 2 + dr
            yy = y - sign[dr] * d
            x_send(k, yy, FIRST, ROWS - FIRST)
            crossed.append((k, yy))

    def near_chunk(c):
        acc = jnp.zeros((256, 256), F32)
        for dx in range(3):
            for dy in range(3):
                lhs = lines(ll, 8 * c + 1 + dx, 8, dy, 2)
                acc = acc + jnp.dot(lhs, near[pl.ds(256 * (3 * dx + dy), 256), :], preferred_element_type=F32)
        near_v[pl.ds(256 * c, 256), :] = acc

    def lower_line(i, _):
        for b in range(2):
            first = jnp.zeros((16, 128), F32)
            second = jnp.zeros((16, 128), F32)
            for k, (dx, dy) in enumerate(OFFSETS):
                base = PITCH * (i + 2 + dx) + 8 + 2 * b + 2 * dy
                real = pf[pl.ds(base, 16, stride=4), :]
                imag = pf[pl.ds(base + 1, 16, stride=4), :]
                t0 = low[pl.ds(2 * k, 1), :]
                t1 = low[pl.ds(2 * k + 1, 1), :]
                first = first + (t0 * real - t1 * imag)
                second = second + (t0 * imag + t1 * real)
            rows = pl.ds(pl.multiple_of(32 * i + 16 * b, 16), 16)
            low_v[rows, pl.ds(0, 128)] = first
            low_v[rows, pl.ds(128, 128)] = second
        return 0

    step(1, 0, 0)
    step(1, 0, 1)
    for x in range(1, WIDE - 1):
        for k in (0, 3):
            plane(x, k)
    step(1, 1, 0)
    step(1, 1, 1)
    near_chunk(0)
    near_chunk(1)
    step(2, 0, 0)
    step(2, 0, 1)
    near_chunk(2)
    near_chunk(3)
    near_copy = pltpu.make_async_copy(near_v, near_out, loc.at[2])
    near_copy.start()
    mask_copy.wait()
    step(2, 1, 0)
    step(2, 1, 1)
    lax.fori_loop(0, TX // 2, lower_line, 0)
    step(3, 0, 0)
    step(3, 0, 1)
    lax.fori_loop(TX // 2, TX, lower_line, 0)
    low_copy = pltpu.make_async_copy(low_v, lower_out, loc.at[3])
    low_copy.start()
    step(3, 1, 0)
    step(3, 1, 1)
    y_wait(0, 3, 0)
    y_wait(1, 3, 0)
    x_send(8, y - 4, FIRST, ROWS - FIRST)
    crossed.append((8, y - 4))
    y_wait(0, 3, 1)
    y_wait(1, 3, 1)
    x_wait(1, y, FIRST, ROWS - FIRST)
    for k, yy in crossed:
        x_wait(k, yy, FIRST, ROWS - FIRST)
    local.wait()
    near_copy.wait()
    low_copy.wait()
    for copy in sent:
        copy.wait_send()


def finish_kernel(
    tile_at,
    kind_at,
    used,
    table,
    group,
    lower_in,
    near_in,
    mask_in,
    p2c,
    recv_map,
    out,
    gb,
    gf,
    ta,
    tb,
    sa,
    sb,
    low_v,
    near_v,
    mask_v,
    sem,
):
    chunks = group.shape[0]
    loads = [pltpu.make_async_copy(group.at[c], gb.at[c], sem.at[c]) for c in range(chunks)]
    rest = [
        pltpu.make_async_copy(src, dst, sem.at[chunks + n])
        for n, (src, dst) in enumerate(((lower_in, low_v), (near_in, near_v), (mask_in, mask_v)))
    ]
    for copy in loads + rest:
        copy.start()

    kinds = table.shape[0] // 4
    zero = jnp.zeros((kinds, 128), F32)
    real = [table[pl.ds(n, kinds, stride=4), :] for n in range(2)]
    imag = [table[pl.ds(2 + n, kinds, stride=4), :] for n in range(2)]
    for par in range(2):
        for row in range(8):
            here = row // 4 == par
            part = row % 4
            at = pl.ds(8 * kinds * par + row, kinds, stride=8)
            ta[at, :] = real[part % 2] if here else zero
            tb[at, :] = (imag[part % 2] if part < 2 else -imag[part % 2]) if here else zero
    ta[pl.ds(16 * kinds, 8), :] = jnp.zeros((8, 128), F32)
    tb[pl.ds(16 * kinds, 8), :] = jnp.zeros((8, 128), F32)

    for c in range(chunks):
        loads[c].wait()
        gf[pl.ds(ROWS * c, ROWS), :] = gb[c].astype(F32)

    def target(t, _):
        def four(q, carry):
            s1, s2 = carry
            for e in range(4):
                at = t * 16 + q * 4 + e
                x = gf[pl.ds(pl.multiple_of(tile_at[at], 8), 8), :]
                kk = pl.multiple_of(kind_at[at], 8)
                s1 = s1 + ta[pl.ds(kk, 8), :] * x
                s2 = s2 + tb[pl.ds(kk, 8), :] * x
            return s1, s2

        zero_tile = jnp.zeros((8, 128), F32)
        s1, s2 = lax.fori_loop(0, used[t], four, (zero_tile, zero_tile))
        rows = pl.ds(pl.multiple_of(8 * t, 8), 8)
        sa[rows, :] = s1
        sb[rows, :] = s2
        return 0

    lax.fori_loop(0, 256, target, 0)

    def take(ref, row):
        return ref[pl.ds(row, 256, stride=8), :] + ref[pl.ds(row + 4, 256, stride=8), :]

    parts = [take(sa, n) + take(sb, (n + 2) % 4) for n in range(4)]
    coarse_in = jnp.concatenate(parts, axis=1).astype(BF16)
    for copy in rest:
        copy.wait()
    for q in range(4):
        got = jnp.dot(coarse_in, p2c[pl.ds(512 * q, 512), :], preferred_element_type=F32)
        for p in range(16):
            rows = pl.ds(64 * p + 16 * q, 16)
            low_v[rows, :] = low_v[rows, :] + got[16 * p : 16 * p + 16]
    for block in range(4):
        rows = pl.ds(256 * block, 256)
        field = jnp.dot(low_v[rows, :].astype(BF16), recv_map[...], preferred_element_type=F32) + near_v[rows, :]
        mask = mask_v[rows, :]
        for h in range(2):
            kept = field[:, 128 * h : 128 * h + 128] * mask
            for n in range(16):
                i = 8 * block + n // 2
                out[pl.ds(64 * i + 2 * (n % 2) + h, 16, stride=4), :] = kept[16 * n : 16 * n + 16]


def body(
    n_gx,
    n_gy,
    currents,
    box_count,
    aggregate,
    near_blocks,
    low_translator,
    child_to_parent,
    coarse_list,
    coarse_kind,
    coarse_count,
    up_translator,
    parent_to_child,
    receive_map,
):
    vmem = pl.BlockSpec(memory_space=pltpu.VMEM)
    smem = pl.BlockSpec(memory_space=pltpu.SMEM)
    anywhere = pl.BlockSpec(memory_space=pl.ANY)
    group, lower, near, mask = pl.pallas_call(
        functools.partial(gather_kernel, n_gx, n_gy),
        name="gather",
        out_shape=(
            jax.ShapeDtypeStruct((n_gy, ROWS, 128), BF16),
            jax.ShapeDtypeStruct((1024, 256), F32),
            jax.ShapeDtypeStruct((1024, 256), F32),
            jax.ShapeDtypeStruct((1024, 128), F32),
        ),
        in_specs=[vmem] * 6,
        out_specs=(anywhere,) * 4,
        scratch_shapes=[
            pltpu.VMEM((2048, 32), BF16),
            pltpu.VMEM((2048, 128), F32),
            pltpu.VMEM((WIDE * PITCH, 128), F32),
            pltpu.VMEM((WIDE * PITCH, 128), F32),
            pltpu.VMEM((WIDE * 64, 256), BF16),
            pltpu.VMEM((1024, 256), BF16),
            pltpu.VMEM((ROWS, 128), F32),
            pltpu.VMEM((ROWS, 128), BF16),
            pltpu.VMEM((WIDE * 8, 128), BF16),
            pltpu.VMEM((WIDE * 8, 128), BF16),
            pltpu.VMEM((WIDE * 8, 128), BF16),
            pltpu.VMEM((WIDE * 8, 128), BF16),
            pltpu.VMEM((1024, 256), F32),
            pltpu.VMEM((1024, 256), F32),
            pltpu.SemaphoreType.DMA((2, 4, 2)),
            pltpu.SemaphoreType.DMA((2, 4, 2)),
            pltpu.SemaphoreType.DMA((9,)),
            pltpu.SemaphoreType.DMA((9,)),
            pltpu.SemaphoreType.DMA((6,)),
            pltpu.SemaphoreType.DMA((6,)),
            pltpu.SemaphoreType.DMA((4,)),
        ],
        compiler_params=pltpu.CompilerParams(
            collective_id=0, has_side_effects=True, vmem_limit_bytes=40 * 1024 * 1024
        ),
    )(
        currents.reshape(2048, 128),
        box_count,
        aggregate,
        near_blocks.reshape(9 * 256, 256),
        low_translator.reshape(32, 128),
        child_to_parent.reshape(1024, 512),
    )

    source = coarse_list.reshape(256, 16)
    tile = (((source >> 4) & 15) << 8) + ((source >> 8) << 4) + (source & 15)
    valid = lax.broadcasted_iota(jnp.int32, (256, 16), 1) < coarse_count.reshape(256, 1)
    kind = coarse_kind.reshape(256, 16) + 64 * (source & 1)
    tile_at = ((tile >> 1) * 8).reshape(4096)
    kind_at = (jnp.where(valid, kind, 128) * 8).reshape(4096)
    used = ((coarse_count + 3) // 4).reshape(256)
    out = pl.pallas_call(
        finish_kernel,
        name="finish",
        out_shape=jax.ShapeDtypeStruct((2048, 128), F32),
        in_specs=[smem, smem, smem, vmem] + [anywhere] * 4 + [vmem, vmem],
        out_specs=vmem,
        scratch_shapes=[
            pltpu.VMEM((n_gy, ROWS, 128), BF16),
            pltpu.VMEM((n_gy * ROWS, 128), F32),
            pltpu.VMEM((129 * 8, 128), F32),
            pltpu.VMEM((129 * 8, 128), F32),
            pltpu.VMEM((2048, 128), F32),
            pltpu.VMEM((2048, 128), F32),
            pltpu.VMEM((1024, 256), F32),
            pltpu.VMEM((1024, 256), F32),
            pltpu.VMEM((1024, 128), F32),
            pltpu.SemaphoreType.DMA((n_gy + 3,)),
        ],
        compiler_params=pltpu.CompilerParams(vmem_limit_bytes=40 * 1024 * 1024),
    )(
        tile_at,
        kind_at,
        used,
        up_translator.reshape(256, 128),
        group,
        lower,
        near,
        mask,
        parent_to_child.reshape(2048, 256),
        receive_map,
    )
    return out.reshape(32, 32, 2, 128)


def solution(mesh):
    in_specs = (
        P("gx", "gy", None, None),
        P("gx", "gy"),
        P(),
        P(),
        P(),
        P(),
        P("gx", "gy", None),
        P("gx", "gy", None),
        P("gx", "gy"),
        P(),
        P(),
        P(),
    )
    out_specs = P("gx", "gy", None, None)
    step = functools.partial(body, mesh.shape["gx"], mesh.shape["gy"])
    return jax.shard_map(step, mesh=mesh, in_specs=in_specs, out_specs=out_specs, check_vma=False)
```

```python
import functools

import jax
import jax.numpy as jnp
from jax import lax
from jax.experimental import pallas as pl
from jax.experimental.pallas import tpu as pltpu
from jax.sharding import PartitionSpec as P

F32 = jnp.float32
BF16 = jnp.bfloat16
MESH = pl.DeviceIdType.MESH
TX = 32
TY = 32
PITCH = 80
WIDE = TX + 4
ROWS = 1024
FIRST = 448
OFFSETS = [(dx, dy) for dx in range(-2, 3) for dy in range(-2, 3) if max(abs(dx), abs(dy)) == 2]


def remote(src, dst, send, recv, device):
    return pltpu.make_async_remote_copy(
        src_ref=src, dst_ref=dst, send_sem=send, recv_sem=recv, device_id=device, device_id_type=MESH
    )


def gather_kernel(
    n_gx,
    n_gy,
    cur_in,
    cnt_in,
    agg_in,
    near_in,
    low_in,
    c2p_in,
    table_in,
    kind_in,
    used_in,
    list_in,
    order,
    tiles,
    factor_r,
    factor_i,
    low_v,
    near_v,
    mask_v,
    cur,
    cnt,
    agg,
    near,
    low,
    c2p,
    table,
    kind,
    used,
    source,
    group,
    tables,
    picks,
    sel_rows,
    cntb,
    lf,
    pf,
    ll,
    pv,
    cf,
    own,
    s_lo,
    s_hi,
    h_lo,
    h_hi,
    ys,
    yr,
    xs,
    xr,
    hs,
    hr,
    ld,
):
    gx = lax.axis_index("gx")
    gy = lax.axis_index("gy")
    ring = n_gy // 2
    y = gy // 2
    xh = lax.rem(gy, 2)
    px = 1 - xh

    def slot(yy, xx):
        return lax.rem(yy + ring, ring) * 2 + xx

    x_next = {"gx": lax.rem(gx + 1, n_gx)}
    x_prev = {"gx": lax.rem(gx + n_gx - 1, n_gx)}
    y_next = {"gy": lax.rem(gy + 1, n_gy)}
    y_prev = {"gy": lax.rem(gy + n_gy - 1, n_gy)}
    r_next = {"gy": slot(y + 1, xh)}
    r_prev = {"gy": slot(y - 1, xh)}
    r_cross = {"gy": slot(y, px)}
    barrier = pltpu.get_barrier_semaphore()
    for device in (x_next, x_prev, y_next, y_prev, r_next, r_prev):
        pl.semaphore_signal(barrier, inc=1, device_id=device, device_id_type=MESH)

    pairs = (
        (cnt_in, cnt),
        (cur_in, cur),
        (agg_in, agg),
        (c2p_in, c2p),
        (table_in, table),
        (kind_in, kind),
        (used_in, used),
        (near_in, near),
        (low_in, low),
        (list_in, source),
    )
    loads = [pltpu.make_async_copy(src, dst, ld.at[n]) for n, (src, dst) in enumerate(pairs)]
    for copy in loads:
        copy.start()
    loads[0].wait()
    loads[1].wait()

    pick = (
        lax.broadcasted_iota(jnp.int32, (2 * TY, TY), 0) // 2 == lax.broadcasted_iota(jnp.int32, (2 * TY, TY), 1)
    ).astype(F32)
    for i in range(TX):
        line = jnp.broadcast_to(cnt[pl.ds(i, 1), :].astype(F32), (2 * TY, TY))
        sel_rows[pl.ds(2 * TY * i, 2 * TY), :] = (line * pick).astype(BF16)
    cntb[...] = jnp.dot(sel_rows[...], jnp.ones((TY, 128), BF16), preferred_element_type=F32)
    lane = lax.broadcasted_iota(jnp.int32, (2 * TY, 128), 1).astype(F32)
    for i in range(TX):
        rows = pl.ds(2 * TY * i, 2 * TY)
        live = jnp.where(lane < cntb[rows, :], cur[rows, :].astype(F32), 0.0)
        lf[pl.ds(PITCH * (i + 2) + 8, 2 * TY), :] = live

    def piece(ref, x, start):
        real = ref[pl.ds(PITCH * x + start, 16, stride=4), :]
        imag = ref[pl.ds(PITCH * x + start + 1, 16, stride=4), :]
        return real, imag

    def plane(x, k):
        real, imag = piece(lf, x, 6 + 2 * k)
        base = 64 * x + 16 * k
        ll[pl.ds(base, 16), :] = jnp.concatenate([real, imag], axis=1).astype(BF16)

    for i in range(TX):
        for k in (1, 2):
            plane(i + 2, k)

    def lines(ref, x, count, k, planes):
        parts = [ref[pl.ds(64 * (x + n) + 16 * k, 16 * planes), :] for n in range(count)]
        return jnp.concatenate(parts, axis=0)

    def spread(x, b, value):
        for h in range(2):
            pf[pl.ds(PITCH * x + 8 + 2 * b + h, 16, stride=4), :] = value[:, 128 * h : 128 * h + 128]

    loads[2].wait()
    for block in range(4):
        got = jnp.dot(lines(ll, 2 + 8 * block, 8, 1, 2), agg[...], preferred_element_type=F32).astype(BF16)
        pv[pl.ds(256 * block, 256), :] = got

    loads[3].wait()
    total = jnp.zeros((256, 512), F32)
    for q in range(4):
        child = jnp.concatenate([pv[pl.ds(64 * p + 16 * q, 16), :] for p in range(16)], axis=0)
        total = total + jnp.dot(child, c2p[pl.ds(256 * q, 256), :], preferred_element_type=F32)
    for q in range(4):
        cf[pl.ds(q, 256, stride=4), :] = total[:, 128 * q : 128 * q + 128]
    own[...] = cf[...].astype(BF16)

    pl.semaphore_wait(barrier, 6)

    sign = (1, -1)
    along = (r_next, r_prev)
    sent = []

    def go(copy):
        copy.start()
        sent.append(copy)

    def span(dr, d, w):
        n = ROWS if w == 0 else FIRST
        if d < 3:
            return 0, n
        return (0, n // 2) if dr == 0 else (n // 2, n - n // 2)

    def y_send(dr, d, w):
        start, n = span(dr, d, w)
        where = group.at[slot(y - sign[dr] * d, xh if w == 0 else px), pl.ds(start, n)]
        src = own.at[pl.ds(start, n)] if (d == 0 and w == 0) else where
        go(remote(src, where, ys.at[dr, d, w], yr.at[dr, d, w], along[dr]))

    def y_wait(dr, d, w):
        start, n = span(dr, d, w)
        where = group.at[slot(y - sign[dr] * (d + 1), xh if w == 0 else px), pl.ds(start, n)]
        remote(where, where, ys.at[dr, d, w], yr.at[dr, d, w], along[dr]).wait_recv()

    def x_send(k, yy, start, n, mine=False):
        where = group.at[slot(yy, xh), pl.ds(start, n)]
        src = own.at[pl.ds(start, n)] if mine else where
        go(remote(src, where, xs.at[k], xr.at[k], r_cross))

    def x_wait(k, yy, start, n):
        where = group.at[slot(yy, px), pl.ds(start, n)]
        remote(where, where, xs.at[k], xr.at[k], r_cross).wait_recv()

    x_send(0, y, 0, FIRST, True)
    y_send(0, 0, 0)
    y_send(1, 0, 0)
    x_send(1, y, FIRST, ROWS - FIRST, True)
    def x_halo(k):
        src = (2, 3, TX, TX + 1)[k]
        dst = (TX + 2, TX + 3, 0, 1)[k]
        return remote(
            lf.at[pl.ds(PITCH * src + 8, 2 * TY)],
            lf.at[pl.ds(PITCH * dst + 8, 2 * TY)],
            hs.at[k],
            hr.at[k],
            x_prev if k < 2 else x_next,
        )

    halo = [x_halo(k) for k in range(4)]
    for copy in halo:
        copy.start()

    def unfold(sl, src, first, count):
        def line(p, _):
            rows = src[pl.ds(pl.multiple_of(64 * p, 64), 64), :].astype(F32)
            tiles[pl.ds(pl.multiple_of(1024 * p + 64 * sl, 64), 64), :] = rows
            return 0

        lax.fori_loop(first // 64, (first + count) // 64, line, 0)

    def unfold_slot(yy, xx, first, count):
        sl = slot(yy, xx)
        unfold(sl, group.at[sl], first, count)

    own_lane = lax.broadcasted_iota(jnp.int32, (16, 128), 1).astype(F32)
    for i in range(TX):
        for b in range(2):
            held = cntb[pl.ds(64 * i + 2 * b, 16, stride=4), :]
            mask_v[pl.ds(32 * i + 16 * b, 16), :] = jnp.where(own_lane < held, 1.0, 0.0)
    for i in range(TX):
        for b in range(2):
            spread(i + 2, b, pv[pl.ds(32 * i + 16 * b, 16), :].astype(F32))

    for copy in halo:
        copy.wait()

    @pl.when(gx == 0)
    def _():
        for x in (0, 1):
            lf[pl.ds(PITCH * x + 8, 2 * TY), :] = jnp.zeros((2 * TY, 128), F32)

    @pl.when(gx == n_gx - 1)
    def _():
        for x in (TX + 2, TX + 3):
            lf[pl.ds(PITCH * x + 8, 2 * TY), :] = jnp.zeros((2 * TY, 128), F32)

    for x in range(0, WIDE, 2):
        for buf, start in ((s_lo, 8), (s_hi, 2 * TY)):
            pair = [lf[pl.ds(PITCH * (x + e) + start, 8), :] for e in range(2)]
            buf[pl.ds(8 * x, 16), :] = jnp.concatenate(pair, axis=0).astype(BF16)
    halo_y = [
        remote(s_lo, h_hi, hs.at[4], hr.at[4], y_prev),
        remote(s_hi, h_lo, hs.at[5], hr.at[5], y_next),
    ]
    for copy in halo_y:
        copy.start()

    for copy in loads[4:]:
        copy.wait()
    kinds = table.shape[0] // 4
    for n in range(4):
        rest = table[pl.ds(2 * (n % 2) + n // 2, kinds, stride=4), :]
        for part in range(3):
            top = rest.astype(BF16)
            tables[pl.ds(kinds * part, kinds), pl.ds(128 * n, 128)] = top
            rest = rest - top.astype(F32)
    square = (lax.broadcasted_iota(jnp.int32, (16, 16), 0) == lax.broadcasted_iota(jnp.int32, (16, 16), 1)).astype(F32)
    spread_used = [jnp.broadcast_to(used[pl.ds(p, 1), :].astype(F32), (16, 16)) * square for p in range(16)]
    held_used = jnp.dot(
        jnp.concatenate(spread_used, axis=0).astype(BF16), jnp.ones((16, 128), BF16), preferred_element_type=F32
    )
    entry = lax.broadcasted_iota(jnp.int32, (256, 16), 1).astype(F32)
    picks[...] = jnp.where(entry < held_used[:, :16], kind[...].astype(F32), -1.0)

    group_of = lax.broadcasted_iota(jnp.int32, (32, 128), 1) // 16
    dense = jnp.zeros((32, 128), jnp.int32)
    for u in range(8):
        some = source[pl.ds(u, 32, stride=8), :]
        dense = jnp.where(group_of == u, jnp.concatenate([some] * 8, axis=1), dense)
    order[...] = dense

    def factor_part(e):
        wide = lax.rem(lax.broadcasted_iota(jnp.int32, (256, 3 * kinds), 1), kinds).astype(F32)
        choice = jnp.broadcast_to(picks[:, e : e + 1], (256, 3 * kinds)) == wide
        got = jnp.dot(jnp.where(choice, 1.0, 0.0).astype(BF16), tables[...], preferred_element_type=F32)
        for row in range(4):
            at = pl.ds(1024 * e + row, 256, stride=4)
            n = row % 2
            factor_r[at, :] = got[:, 128 * n : 128 * n + 128]
            part = got[:, 256 + 128 * n : 384 + 128 * n]
            factor_i[at, :] = -part if row >= 2 else part

    x_wait(0, y, 0, FIRST)
    y_send(0, 0, 1)
    y_send(1, 0, 1)
    unfold(gy, own, 0, ROWS)
    unfold_slot(y, px, 0, FIRST)
    factor_part(0)
    factor_part(1)

    for x in (0, 1, TX + 2, TX + 3):
        for k in (1, 2):
            plane(x, k)
    for x in (0, TX + 2):
        got = jnp.dot(lines(ll, x, 2, 1, 2), agg[...], preferred_element_type=F32).astype(BF16).astype(F32)
        for e in range(2):
            for b in range(2):
                spread(x + e, b, got[32 * e + 16 * b : 32 * e + 16 * b + 16])

    for copy in halo_y:
        copy.wait()

    @pl.when(gy == 0)
    def _():
        h_lo[...] = jnp.zeros_like(h_lo)

    @pl.when(gy == n_gy - 1)
    def _():
        h_hi[...] = jnp.zeros_like(h_hi)

    for x in range(0, WIDE, 2):
        for buf, start in ((h_lo, 0), (h_hi, 2 * TY + 8)):
            pair = buf[pl.ds(8 * x, 16), :].astype(F32)
            for e in range(2):
                lf[pl.ds(PITCH * (x + e) + start, 8), :] = pair[8 * e : 8 * e + 8]

    for start in (4, 6, 2 * TY + 8, 2 * TY + 10):
        cols = [lf[pl.ds(start + h, WIDE, stride=PITCH), :] for h in range(2)]
        lhs = jnp.concatenate(cols, axis=1)
        lhs = jnp.concatenate([lhs, jnp.zeros((48 - WIDE, 256), F32)], axis=0).astype(BF16)
        got = jnp.dot(lhs, agg[...], preferred_element_type=F32).astype(BF16).astype(F32)
        for h in range(2):
            pf[pl.ds(start + h, WIDE, stride=PITCH), :] = got[:WIDE, 128 * h : 128 * h + 128]

    crossed = []

    def step(d, w, dr):
        y_wait(dr, d - 1, w)
        y_send(dr, d, w)
        yy = y - sign[dr] * d
        if w == 0:
            k = 2 + (d - 1) * 2 + dr
            x_send(k, yy, FIRST, ROWS - FIRST)
            crossed.append((k, yy))
            unfold_slot(yy, xh, 0, ROWS)
        else:
            unfold_slot(yy, px, 0, FIRST)

    def cross_step(n):
        k, yy = crossed[n]
        x_wait(k, yy, FIRST, ROWS - FIRST)
        unfold_slot(yy, px, FIRST, ROWS - FIRST)

    def near_chunk(c):
        acc = jnp.zeros((256, 256), F32)
        for dx in range(3):
            for dy in range(3):
                lhs = lines(ll, 8 * c + 1 + dx, 8, dy, 2)
                acc = acc + jnp.dot(lhs, near[pl.ds(256 * (3 * dx + dy), 256), :], preferred_element_type=F32)
        near_v[pl.ds(256 * c, 256), :] = acc

    def lower_line(i, _):
        for b in range(2):
            first = jnp.zeros((16, 128), F32)
            second = jnp.zeros((16, 128), F32)
            for k, (dx, dy) in enumerate(OFFSETS):
                base = PITCH * (i + 2 + dx) + 8 + 2 * b + 2 * dy
                real = pf[pl.ds(base, 16, stride=4), :]
                imag = pf[pl.ds(base + 1, 16, stride=4), :]
                t0 = low[pl.ds(2 * k, 1), :]
                t1 = low[pl.ds(2 * k + 1, 1), :]
                first = first + (t0 * real - t1 * imag)
                second = second + (t0 * imag + t1 * real)
            rows = pl.ds(pl.multiple_of(32 * i + 16 * b, 16), 16)
            low_v[rows, pl.ds(0, 128)] = first
            low_v[rows, pl.ds(128, 128)] = second
        return 0

    def factor_parts(n):
        factor_part(2 * n)
        factor_part(2 * n + 1)

    crossed.append((1, y))
    step(1, 0, 0)
    step(1, 0, 1)
    for x in range(1, WIDE - 1):
        for k in (0, 3):
            plane(x, k)
    factor_parts(1)
    step(1, 1, 0)
    step(1, 1, 1)
    near_chunk(0)
    near_chunk(1)
    factor_parts(2)
    cross_step(0)
    step(2, 0, 0)
    step(2, 0, 1)
    near_chunk(2)
    near_chunk(3)
    factor_parts(3)
    cross_step(1)
    cross_step(2)
    step(2, 1, 0)
    step(2, 1, 1)
    lax.fori_loop(0, TX // 2, lower_line, 0)
    factor_parts(4)
    step(3, 0, 0)
    step(3, 0, 1)
    cross_step(3)
    cross_step(4)
    lax.fori_loop(TX // 2, TX, lower_line, 0)
    factor_parts(5)
    step(3, 1, 0)
    step(3, 1, 1)
    factor_parts(6)
    y_wait(0, 3, 0)
    y_wait(1, 3, 0)
    x_send(8, y - 4, FIRST, ROWS - FIRST)
    crossed.append((8, y - 4))
    unfold_slot(y - 4, xh, 0, ROWS)
    factor_parts(7)
    cross_step(5)
    cross_step(6)
    y_wait(0, 3, 1)
    y_wait(1, 3, 1)
    unfold_slot(y - 4, px, 0, FIRST)
    cross_step(7)
    for copy in sent:
        copy.wait_send()


def finish_kernel(order, tiles, factor_r, factor_i, low_v, near_v, mask_v, p2c_in, recv_in, out, sums, incoming, p2c, recv_map, sem):
    loads = [pltpu.make_async_copy(p2c_in, p2c, sem.at[0]), pltpu.make_async_copy(recv_in, recv_map, sem.at[1])]
    for copy in loads:
        copy.start()

    def targets(n, _):
        for u in range(8):
            t = 8 * n + u
            first = jnp.zeros((4, 128), F32)
            second = jnp.zeros((4, 128), F32)
            for e in range(16):
                x = tiles[order[n, 16 * u + e]]
                first = first + factor_r[t + 256 * e] * x
                second = second + factor_i[t + 256 * e] * x
            rows = pl.multiple_of(8 * t, 8)
            sums[pl.ds(rows, 4), :] = first
            sums[pl.ds(rows + 4, 4), :] = second
        return 0

    lax.fori_loop(0, 32, targets, 0)

    def take(row):
        return sums[pl.ds(row, 256, stride=8), :]

    parts = [take(0) + take(6), take(1) + take(7), take(2) + take(4), take(3) + take(5)]
    coarse_in = jnp.concatenate(parts, axis=1).astype(BF16)
    for copy in loads:
        copy.wait()
    for q in range(4):
        got = jnp.dot(coarse_in, p2c[pl.ds(512 * q, 512), :], preferred_element_type=F32)
        for p in range(16):
            rows = pl.ds(64 * p + 16 * q, 16)
            incoming[rows, :] = (low_v[rows, :] + got[16 * p : 16 * p + 16]).astype(BF16)
    for block in range(4):
        rows = pl.ds(256 * block, 256)
        field = jnp.dot(incoming[rows, :], recv_map[...], preferred_element_type=F32) + near_v[rows, :]
        mask = mask_v[rows, :]
        for h in range(2):
            kept = field[:, 128 * h : 128 * h + 128] * mask
            for n in range(16):
                i = 8 * block + n // 2
                out[pl.ds(64 * i + 2 * (n % 2) + h, 16, stride=4), :] = kept[16 * n : 16 * n + 16]


def body(
    n_gx,
    n_gy,
    currents,
    box_count,
    aggregate,
    near_blocks,
    low_translator,
    child_to_parent,
    coarse_list,
    coarse_kind,
    coarse_count,
    up_translator,
    parent_to_child,
    receive_map,
):
    vmem = pltpu.VMEM
    held = pl.BlockSpec(memory_space=pltpu.HBM)
    near_by = pl.BlockSpec(memory_space=pltpu.VMEM)
    order, tiles, factor_r, factor_i, lower, near, mask = pl.pallas_call(
        functools.partial(gather_kernel, n_gx, n_gy),
        name="gather",
        out_shape=(
            jax.ShapeDtypeStruct((32, 128), jnp.int32),
            jax.ShapeDtypeStruct((16384, 128), F32),
            jax.ShapeDtypeStruct((16384, 128), F32),
            jax.ShapeDtypeStruct((16384, 128), F32),
            jax.ShapeDtypeStruct((1024, 256), F32),
            jax.ShapeDtypeStruct((1024, 256), F32),
            jax.ShapeDtypeStruct((1024, 128), F32),
        ),
        in_specs=[held] * 10,
        out_specs=(near_by,) * 7,
        scratch_shapes=[
            vmem((2048, 128), BF16),
            vmem((32, 32), jnp.int32),
            vmem((256, 256), BF16),
            vmem((2304, 256), BF16),
            vmem((32, 128), F32),
            vmem((1024, 512), BF16),
            vmem((256, 128), F32),
            vmem((256, 16), jnp.int32),
            vmem((16, 16), jnp.int32),
            vmem((256, 16), jnp.int32),
            vmem((n_gy, ROWS, 128), BF16),
            vmem((192, 512), BF16),
            vmem((256, 16), F32),
            vmem((2048, 32), BF16),
            vmem((2048, 128), F32),
            vmem((WIDE * PITCH, 128), F32),
            vmem((WIDE * PITCH, 128), F32),
            vmem((WIDE * 64, 256), BF16),
            vmem((1024, 256), BF16),
            vmem((ROWS, 128), F32),
            vmem((ROWS, 128), BF16),
            vmem((WIDE * 8, 128), BF16),
            vmem((WIDE * 8, 128), BF16),
            vmem((WIDE * 8, 128), BF16),
            vmem((WIDE * 8, 128), BF16),
            pltpu.SemaphoreType.DMA((2, 4, 2)),
            pltpu.SemaphoreType.DMA((2, 4, 2)),
            pltpu.SemaphoreType.DMA((9,)),
            pltpu.SemaphoreType.DMA((9,)),
            pltpu.SemaphoreType.DMA((6,)),
            pltpu.SemaphoreType.DMA((6,)),
            pltpu.SemaphoreType.DMA((10,)),
        ],
        compiler_params=pltpu.CompilerParams(
            collective_id=0, has_side_effects=True, vmem_limit_bytes=16 * 1024 * 1024
        ),
    )(
        *(
            pltpu.with_memory_space_constraint(array, pltpu.HBM)
            for array in (
                currents.reshape(2048, 128),
                box_count,
                aggregate,
                near_blocks.reshape(2304, 256),
                low_translator.reshape(32, 128),
                child_to_parent.reshape(1024, 512),
                up_translator.reshape(64, 2, 2, 128).transpose(0, 2, 1, 3).reshape(256, 128),
                coarse_kind.reshape(256, 16),
                coarse_count,
                coarse_list.reshape(256, 16),
            )
        )
    )
    out = pl.pallas_call(
        finish_kernel,
        name="finish",
        out_shape=jax.ShapeDtypeStruct((2048, 128), F32),
        in_specs=[pl.BlockSpec(memory_space=pltpu.SMEM)] + [near_by] * 6 + [held] * 2,
        out_specs=near_by,
        scratch_shapes=[
            vmem((2048, 128), F32),
            vmem((1024, 256), BF16),
            vmem((2048, 256), BF16),
            vmem((256, 256), BF16),
            pltpu.SemaphoreType.DMA((2,)),
        ],
        compiler_params=pltpu.CompilerParams(vmem_limit_bytes=6 * 1024 * 1024),
    )(
        order,
        tiles.reshape(4096, 4, 128),
        factor_r.reshape(4096, 4, 128),
        factor_i.reshape(4096, 4, 128),
        lower,
        near,
        mask,
        pltpu.with_memory_space_constraint(parent_to_child.reshape(2048, 256), pltpu.HBM),
        pltpu.with_memory_space_constraint(receive_map, pltpu.HBM),
    )
    return out.reshape(32, 32, 2, 128)


def solution(mesh):
    in_specs = (
        P("gx", "gy", None, None),
        P("gx", "gy"),
        P(),
        P(),
        P(),
        P(),
        P("gx", "gy", None),
        P("gx", "gy", None),
        P("gx", "gy"),
        P(),
        P(),
        P(),
    )
    out_specs = P("gx", "gy", None, None)
    step = functools.partial(body, mesh.shape["gx"], mesh.shape["gy"])
    return jax.shard_map(step, mesh=mesh, in_specs=in_specs, out_specs=out_specs, check_vma=False)
```

```python
import functools

import jax
import jax.numpy as jnp
from jax import lax
from jax.experimental import pallas as pl
from jax.experimental.pallas import tpu as pltpu
from jax.sharding import PartitionSpec as P

F32 = jnp.float32
BF16 = jnp.bfloat16
MESH = pl.DeviceIdType.MESH
TX = 32
TY = 32
PITCH = 80
WIDE = TX + 4
ROWS = 1024
FIRST = 448
HALF = FIRST // 2
REST = (ROWS - FIRST) // 2
OWN = ((FIRST, REST), (FIRST + REST, REST), (0, HALF), (HALF, HALF))
OTHER = ((0, HALF), (HALF, HALF))
OFFSETS = [(dx, dy) for dx in range(-2, 3) for dy in range(-2, 3) if max(abs(dx), abs(dy)) == 2]


def remote(src, dst, send, recv, device):
    return pltpu.make_async_remote_copy(
        src_ref=src, dst_ref=dst, send_sem=send, recv_sem=recv, device_id=device, device_id_type=MESH
    )


def gather_kernel(
    n_gx,
    n_gy,
    cur_in,
    cnt_in,
    agg_in,
    near_in,
    low_in,
    c2p_in,
    table_in,
    kind_in,
    used_in,
    list_in,
    order,
    tiles,
    factor_r,
    factor_i,
    low_v,
    near_v,
    mask_v,
    cur,
    cnt,
    agg,
    near,
    low,
    c2p,
    table,
    kind,
    used,
    source,
    group,
    tables,
    picks,
    sel_rows,
    cntb,
    lf,
    pf,
    ll,
    pv,
    cf,
    own,
    s_lo,
    s_hi,
    h_lo,
    h_hi,
    ys,
    yr,
    xs,
    xr,
    hs,
    hr,
    ld,
):
    gx = lax.axis_index("gx")
    gy = lax.axis_index("gy")
    ring = n_gy // 2
    y = gy // 2
    xh = lax.rem(gy, 2)
    px = 1 - xh

    def slot(yy, xx):
        return lax.rem(yy + ring, ring) * 2 + xx

    x_next = {"gx": lax.rem(gx + 1, n_gx)}
    x_prev = {"gx": lax.rem(gx + n_gx - 1, n_gx)}
    y_next = {"gy": lax.rem(gy + 1, n_gy)}
    y_prev = {"gy": lax.rem(gy + n_gy - 1, n_gy)}
    r_next = {"gy": slot(y + 1, xh)}
    r_prev = {"gy": slot(y - 1, xh)}
    r_cross = {"gy": slot(y, px)}
    barrier = pltpu.get_barrier_semaphore()
    for device in (x_next, x_prev, y_next, y_prev, r_next, r_prev):
        pl.semaphore_signal(barrier, inc=1, device_id=device, device_id_type=MESH)

    pairs = (
        (cnt_in, cnt),
        (cur_in, cur),
        (agg_in, agg),
        (c2p_in, c2p),
        (table_in, table),
        (kind_in, kind),
        (used_in, used),
        (near_in, near),
        (low_in, low),
        (list_in, source),
    )
    loads = [pltpu.make_async_copy(src, dst, ld.at[n]) for n, (src, dst) in enumerate(pairs)]
    for copy in loads[:4]:
        copy.start()
    loads[0].wait()
    loads[1].wait()
    for copy in loads[4:]:
        copy.start()

    pick = (
        lax.broadcasted_iota(jnp.int32, (2 * TY, TY), 0) // 2 == lax.broadcasted_iota(jnp.int32, (2 * TY, TY), 1)
    ).astype(F32)
    for i in range(TX):
        line = jnp.broadcast_to(cnt[pl.ds(i, 1), :].astype(F32), (2 * TY, TY))
        sel_rows[pl.ds(2 * TY * i, 2 * TY), :] = (line * pick).astype(BF16)
    cntb[...] = jnp.dot(sel_rows[...], jnp.ones((TY, 128), BF16), preferred_element_type=F32)
    lane = lax.broadcasted_iota(jnp.int32, (2 * TY, 128), 1).astype(F32)
    for i in range(TX):
        rows = pl.ds(2 * TY * i, 2 * TY)
        live = jnp.where(lane < cntb[rows, :], cur[rows, :].astype(F32), 0.0)
        lf[pl.ds(PITCH * (i + 2) + 8, 2 * TY), :] = live

    def piece(ref, x, start):
        real = ref[pl.ds(PITCH * x + start, 16, stride=4), :]
        imag = ref[pl.ds(PITCH * x + start + 1, 16, stride=4), :]
        return real, imag

    def plane(x, k):
        real, imag = piece(lf, x, 6 + 2 * k)
        base = 64 * x + 16 * k
        ll[pl.ds(base, 16), :] = jnp.concatenate([real, imag], axis=1).astype(BF16)

    for i in range(TX):
        for k in (1, 2):
            plane(i + 2, k)

    def lines(ref, x, count, k, planes):
        parts = [ref[pl.ds(64 * (x + n) + 16 * k, 16 * planes), :] for n in range(count)]
        return jnp.concatenate(parts, axis=0)

    def spread(x, b, value):
        for h in range(2):
            pf[pl.ds(PITCH * x + 8 + 2 * b + h, 16, stride=4), :] = value[:, 128 * h : 128 * h + 128]

    loads[2].wait()
    for block in range(4):
        got = jnp.dot(lines(ll, 2 + 8 * block, 8, 1, 2), agg[...], preferred_element_type=F32).astype(BF16)
        pv[pl.ds(256 * block, 256), :] = got

    loads[3].wait()
    total = jnp.zeros((256, 512), F32)
    for q in range(4):
        child = jnp.concatenate([pv[pl.ds(64 * p + 16 * q, 16), :] for p in range(16)], axis=0)
        total = total + jnp.dot(child, c2p[pl.ds(256 * q, 256), :], preferred_element_type=F32)
    for q in range(4):
        cf[pl.ds(q, 256, stride=4), :] = total[:, 128 * q : 128 * q + 128]
    own[...] = cf[...].astype(BF16)

    pl.semaphore_wait(barrier, 6)

    sign = (1, -1)
    along = (r_next, r_prev)
    sent = []

    def go(copy):
        copy.start()
        sent.append(copy)

    def y_copy(dr, d, w, i, mine=False):
        start, n = (OTHER if w else OWN)[i]
        where = group.at[slot(y - sign[dr] * d, px if w else xh), pl.ds(start, n)]
        k = i + len(OWN) * w
        src = own.at[pl.ds(start, n)] if mine else where
        return remote(src, where, ys.at[dr, d, k], yr.at[dr, d, k], along[dr])

    def y_arrival(dr, d, w, i):
        start, n = (OTHER if w else OWN)[i]
        where = group.at[slot(y - sign[dr] * (d + 1), px if w else xh), pl.ds(start, n)]
        k = i + len(OWN) * w
        return remote(where, where, ys.at[dr, d, k], yr.at[dr, d, k], along[dr])

    def turns(d, i):
        return (0, 1) if d < 3 else (i % 2,)

    def x_copy(j, yy, k, piece, mine=False):
        where = group.at[slot(yy, xh), pl.ds(*piece)]
        src = own.at[pl.ds(*piece)] if mine else where
        return remote(src, where, xs.at[j, k], xr.at[j, k], r_cross)

    def x_arrival(j, yy, k, piece):
        where = group.at[slot(yy, px), pl.ds(*piece)]
        return remote(where, where, xs.at[j, k], xr.at[j, k], r_cross)

    def number(d, dr):
        return 0 if d == 0 else 7 if d == 4 else 1 + 2 * (d - 1) + dr

    for i in range(len(OTHER)):
        go(x_copy(0, y, 2 + i, OTHER[i], True))
    for i in range(len(OWN)):
        for dr in range(2):
            go(y_copy(dr, 0, 0, i, True))
    for i in range(2):
        go(x_copy(0, y, i, OWN[i], True))

    def x_halo(k):
        src = (2, 3, TX, TX + 1)[k]
        dst = (TX + 2, TX + 3, 0, 1)[k]
        return remote(
            lf.at[pl.ds(PITCH * src + 8, 2 * TY)],
            lf.at[pl.ds(PITCH * dst + 8, 2 * TY)],
            hs.at[k],
            hr.at[k],
            x_prev if k < 2 else x_next,
        )

    halo = [x_halo(k) for k in range(4)]
    for copy in halo:
        copy.start()

    def unfold(sl, src, first, count):
        def line(p, _):
            rows = src[pl.ds(pl.multiple_of(64 * p, 64), 64), :].astype(F32)
            tiles[pl.ds(pl.multiple_of(1024 * p + 64 * sl, 64), 64), :] = rows
            return 0

        lax.fori_loop(first // 64, (first + count) // 64, line, 0)

    def unfold_slot(yy, xx, first, count):
        sl = slot(yy, xx)
        unfold(sl, group.at[sl], first, count)

    own_lane = lax.broadcasted_iota(jnp.int32, (16, 128), 1).astype(F32)
    for i in range(TX):
        for b in range(2):
            held = cntb[pl.ds(64 * i + 2 * b, 16, stride=4), :]
            mask_v[pl.ds(32 * i + 16 * b, 16), :] = jnp.where(own_lane < held, 1.0, 0.0)
    for i in range(TX):
        for b in range(2):
            spread(i + 2, b, pv[pl.ds(32 * i + 16 * b, 16), :].astype(F32))

    for copy in halo:
        copy.wait()

    @pl.when(gx == 0)
    def _():
        for x in (0, 1):
            lf[pl.ds(PITCH * x + 8, 2 * TY), :] = jnp.zeros((2 * TY, 128), F32)

    @pl.when(gx == n_gx - 1)
    def _():
        for x in (TX + 2, TX + 3):
            lf[pl.ds(PITCH * x + 8, 2 * TY), :] = jnp.zeros((2 * TY, 128), F32)

    for x in range(0, WIDE, 2):
        for buf, start in ((s_lo, 8), (s_hi, 2 * TY)):
            pair = [lf[pl.ds(PITCH * (x + e) + start, 8), :] for e in range(2)]
            buf[pl.ds(8 * x, 16), :] = jnp.concatenate(pair, axis=0).astype(BF16)
    halo_y = [
        remote(s_lo, h_hi, hs.at[4], hr.at[4], y_prev),
        remote(s_hi, h_lo, hs.at[5], hr.at[5], y_next),
    ]
    for copy in halo_y:
        copy.start()

    for copy in loads[4:]:
        copy.wait()
    kinds = table.shape[0] // 4
    for n in range(4):
        rest = table[pl.ds(2 * (n % 2) + n // 2, kinds, stride=4), :]
        for part in range(3):
            top = rest.astype(BF16)
            tables[pl.ds(kinds * part, kinds), pl.ds(128 * n, 128)] = top
            rest = rest - top.astype(F32)
    square = (lax.broadcasted_iota(jnp.int32, (16, 16), 0) == lax.broadcasted_iota(jnp.int32, (16, 16), 1)).astype(F32)
    spread_used = [jnp.broadcast_to(used[pl.ds(p, 1), :].astype(F32), (16, 16)) * square for p in range(16)]
    held_used = jnp.dot(
        jnp.concatenate(spread_used, axis=0).astype(BF16), jnp.ones((16, 128), BF16), preferred_element_type=F32
    )
    entry = lax.broadcasted_iota(jnp.int32, (256, 16), 1).astype(F32)
    picks[...] = jnp.where(entry < held_used[:, :16], kind[...].astype(F32), -1.0)

    group_of = lax.broadcasted_iota(jnp.int32, (32, 128), 1) // 16
    dense = jnp.zeros((32, 128), jnp.int32)
    for u in range(8):
        some = source[pl.ds(u, 32, stride=8), :]
        dense = jnp.where(group_of == u, jnp.concatenate([some] * 8, axis=1), dense)
    order[...] = dense

    def factor_part(e):
        wide = lax.rem(lax.broadcasted_iota(jnp.int32, (256, 3 * kinds), 1), kinds).astype(F32)
        choice = jnp.broadcast_to(picks[:, e : e + 1], (256, 3 * kinds)) == wide
        got = jnp.dot(jnp.where(choice, 1.0, 0.0).astype(BF16), tables[...], preferred_element_type=F32)
        for row in range(4):
            at = pl.ds(1024 * e + row, 256, stride=4)
            n = row % 2
            factor_r[at, :] = got[:, 128 * n : 128 * n + 128]
            part = got[:, 256 + 128 * n : 384 + 128 * n]
            factor_i[at, :] = -part if row >= 2 else part

    def own_step(d):
        for i in range(len(OWN)):
            for dr in turns(d - 1, i):
                y_arrival(dr, d - 1, 0, i).wait_recv()
                if i < 2:
                    go(x_copy(number(d, dr), y - sign[dr] * d, i, OWN[i]))
            if d < 4:
                for dr in turns(d, i):
                    go(y_copy(dr, d, 0, i))
        for dr in range(2 if d < 4 else 1):
            unfold_slot(y - sign[dr] * d, xh, 0, ROWS)

    def other_step(d):
        for i in range(len(OTHER)):
            if d == 0:
                x_arrival(0, y, 2 + i, OTHER[i]).wait_recv()
            else:
                for dr in turns(d - 1, i):
                    y_arrival(dr, d - 1, 1, i).wait_recv()
            if d < 4:
                for dr in turns(d, i):
                    go(y_copy(dr, d, 1, i))
        for dr in range(2 if 0 < d < 4 else 1):
            unfold_slot(y - sign[dr] * d, px, 0, FIRST)

    def cross_step(d):
        for i in range(2):
            for dr in (0,) if d == 0 else turns(d - 1, i):
                x_arrival(number(d, dr), y - sign[dr] * d, i, OWN[i]).wait_recv()
        for dr in range(2 if 0 < d < 4 else 1):
            unfold_slot(y - sign[dr] * d, px, FIRST, ROWS - FIRST)

    unfold(gy, own, 0, ROWS)
    for e in range(4):
        factor_part(e)
    own_step(1)
    other_step(0)

    for x in (0, 1, TX + 2, TX + 3):
        for k in (1, 2):
            plane(x, k)
    for x in (0, TX + 2):
        got = jnp.dot(lines(ll, x, 2, 1, 2), agg[...], preferred_element_type=F32).astype(BF16).astype(F32)
        for e in range(2):
            for b in range(2):
                spread(x + e, b, got[32 * e + 16 * b : 32 * e + 16 * b + 16])

    for copy in halo_y:
        copy.wait()

    @pl.when(gy == 0)
    def _():
        h_lo[...] = jnp.zeros_like(h_lo)

    @pl.when(gy == n_gy - 1)
    def _():
        h_hi[...] = jnp.zeros_like(h_hi)

    for x in range(0, WIDE, 2):
        for buf, start in ((h_lo, 0), (h_hi, 2 * TY + 8)):
            pair = buf[pl.ds(8 * x, 16), :].astype(F32)
            for e in range(2):
                lf[pl.ds(PITCH * (x + e) + start, 8), :] = pair[8 * e : 8 * e + 8]

    for start in (4, 6, 2 * TY + 8, 2 * TY + 10):
        cols = [lf[pl.ds(start + h, WIDE, stride=PITCH), :] for h in range(2)]
        lhs = jnp.concatenate(cols, axis=1)
        lhs = jnp.concatenate([lhs, jnp.zeros((48 - WIDE, 256), F32)], axis=0).astype(BF16)
        got = jnp.dot(lhs, agg[...], preferred_element_type=F32).astype(BF16).astype(F32)
        for h in range(2):
            pf[pl.ds(start + h, WIDE, stride=PITCH), :] = got[:WIDE, 128 * h : 128 * h + 128]

    def near_chunk(c):
        acc = jnp.zeros((256, 256), F32)
        for dx in range(3):
            for dy in range(3):
                lhs = lines(ll, 8 * c + 1 + dx, 8, dy, 2)
                acc = acc + jnp.dot(lhs, near[pl.ds(256 * (3 * dx + dy), 256), :], preferred_element_type=F32)
        near_v[pl.ds(256 * c, 256), :] = acc

    def lower_line(i, _):
        for b in range(2):
            first = jnp.zeros((16, 128), F32)
            second = jnp.zeros((16, 128), F32)
            for k, (dx, dy) in enumerate(OFFSETS):
                base = PITCH * (i + 2 + dx) + 8 + 2 * b + 2 * dy
                real = pf[pl.ds(base, 16, stride=4), :]
                imag = pf[pl.ds(base + 1, 16, stride=4), :]
                t0 = low[pl.ds(2 * k, 1), :]
                t1 = low[pl.ds(2 * k + 1, 1), :]
                first = first + (t0 * real - t1 * imag)
                second = second + (t0 * imag + t1 * real)
            rows = pl.ds(pl.multiple_of(32 * i + 16 * b, 16), 16)
            low_v[rows, pl.ds(0, 128)] = first
            low_v[rows, pl.ds(128, 128)] = second
        return 0

    for x in range(1, WIDE - 1):
        for k in (0, 3):
            plane(x, k)
    near_chunk(0)
    near_chunk(1)
    factor_part(4)
    factor_part(5)
    own_step(2)
    other_step(1)
    cross_step(0)
    near_chunk(2)
    near_chunk(3)
    for e in range(6, 9):
        factor_part(e)
    cross_step(1)
    own_step(3)
    other_step(2)
    lax.fori_loop(0, TX // 2, lower_line, 0)
    for e in range(9, 12):
        factor_part(e)
    cross_step(2)
    own_step(4)
    other_step(3)
    lax.fori_loop(TX // 2, TX, lower_line, 0)
    for e in range(12, 16):
        factor_part(e)
    cross_step(3)
    other_step(4)
    cross_step(4)
    for copy in sent:
        copy.wait_send()


def finish_kernel(order, tiles, factor_r, factor_i, low_v, near_v, mask_v, p2c_in, recv_in, result, sums, incoming, p2c, recv_map, out, sem):
    loads = [pltpu.make_async_copy(p2c_in, p2c, sem.at[0]), pltpu.make_async_copy(recv_in, recv_map, sem.at[1])]
    for copy in loads:
        copy.start()

    def targets(n, _):
        for u in range(8):
            t = 8 * n + u
            first = jnp.zeros((4, 128), F32)
            second = jnp.zeros((4, 128), F32)
            for e in range(16):
                x = tiles[order[n, 16 * u + e]]
                first = first + factor_r[t + 256 * e] * x
                second = second + factor_i[t + 256 * e] * x
            rows = pl.multiple_of(8 * t, 8)
            sums[pl.ds(rows, 4), :] = first
            sums[pl.ds(rows + 4, 4), :] = second
        return 0

    lax.fori_loop(0, 32, targets, 0)

    def take(row):
        return sums[pl.ds(row, 256, stride=8), :]

    parts = [take(0) + take(6), take(1) + take(7), take(2) + take(4), take(3) + take(5)]
    coarse_in = jnp.concatenate(parts, axis=1).astype(BF16)
    for copy in loads:
        copy.wait()
    for q in range(4):
        got = jnp.dot(coarse_in, p2c[pl.ds(512 * q, 512), :], preferred_element_type=F32)
        for p in range(16):
            rows = pl.ds(64 * p + 16 * q, 16)
            incoming[rows, :] = (low_v[rows, :] + got[16 * p : 16 * p + 16]).astype(BF16)
    for block in range(4):
        rows = pl.ds(256 * block, 256)
        field = jnp.dot(incoming[rows, :], recv_map[...], preferred_element_type=F32) + near_v[rows, :]
        mask = mask_v[rows, :]
        for h in range(2):
            kept = field[:, 128 * h : 128 * h + 128] * mask
            for n in range(16):
                i = 8 * block + n // 2
                out[pl.ds(64 * i + 2 * (n % 2) + h, 16, stride=4), :] = kept[16 * n : 16 * n + 16]
        done = pltpu.make_async_copy(
            out.at[pl.ds(512 * block, 512)], result.at[pl.ds(512 * block, 512)], sem.at[2 + block]
        )
        done.start()
        loads.append(done)
    for copy in loads[2:]:
        copy.wait()


def body(
    n_gx,
    n_gy,
    currents,
    box_count,
    aggregate,
    near_blocks,
    low_translator,
    child_to_parent,
    coarse_list,
    coarse_kind,
    coarse_count,
    up_translator,
    parent_to_child,
    receive_map,
):
    vmem = pltpu.VMEM
    held = pl.BlockSpec(memory_space=pltpu.HBM)
    near_by = pl.BlockSpec(memory_space=pltpu.VMEM)
    order, tiles, factor_r, factor_i, lower, near, mask = pl.pallas_call(
        functools.partial(gather_kernel, n_gx, n_gy),
        name="gather",
        out_shape=(
            jax.ShapeDtypeStruct((32, 128), jnp.int32),
            jax.ShapeDtypeStruct((16384, 128), F32),
            jax.ShapeDtypeStruct((16384, 128), F32),
            jax.ShapeDtypeStruct((16384, 128), F32),
            jax.ShapeDtypeStruct((1024, 256), F32),
            jax.ShapeDtypeStruct((1024, 256), F32),
            jax.ShapeDtypeStruct((1024, 128), F32),
        ),
        in_specs=[held] * 10,
        out_specs=(near_by,) * 7,
        scratch_shapes=[
            vmem((2048, 128), BF16),
            vmem((32, 32), jnp.int32),
            vmem((256, 256), BF16),
            vmem((2304, 256), BF16),
            vmem((32, 128), F32),
            vmem((1024, 512), BF16),
            vmem((256, 128), F32),
            vmem((256, 16), jnp.int32),
            vmem((16, 16), jnp.int32),
            vmem((256, 16), jnp.int32),
            vmem((n_gy, ROWS, 128), BF16),
            vmem((192, 512), BF16),
            vmem((256, 16), F32),
            vmem((2048, 32), BF16),
            vmem((2048, 128), F32),
            vmem((WIDE * PITCH, 128), F32),
            vmem((WIDE * PITCH, 128), F32),
            vmem((WIDE * 64, 256), BF16),
            vmem((1024, 256), BF16),
            vmem((ROWS, 128), F32),
            vmem((ROWS, 128), BF16),
            vmem((WIDE * 8, 128), BF16),
            vmem((WIDE * 8, 128), BF16),
            vmem((WIDE * 8, 128), BF16),
            vmem((WIDE * 8, 128), BF16),
            pltpu.SemaphoreType.DMA((2, 4, 6)),
            pltpu.SemaphoreType.DMA((2, 4, 6)),
            pltpu.SemaphoreType.DMA((8, 4)),
            pltpu.SemaphoreType.DMA((8, 4)),
            pltpu.SemaphoreType.DMA((6,)),
            pltpu.SemaphoreType.DMA((6,)),
            pltpu.SemaphoreType.DMA((10,)),
        ],
        compiler_params=pltpu.CompilerParams(
            collective_id=0, has_side_effects=True, vmem_limit_bytes=16 * 1024 * 1024
        ),
    )(
        *(
            pltpu.with_memory_space_constraint(array, pltpu.HBM)
            for array in (
                currents.reshape(2048, 128),
                box_count,
                aggregate,
                near_blocks.reshape(2304, 256),
                low_translator.reshape(32, 128),
                child_to_parent.reshape(1024, 512),
                up_translator.reshape(64, 2, 2, 128).transpose(0, 2, 1, 3).reshape(256, 128),
                coarse_kind.reshape(256, 16),
                coarse_count,
                coarse_list.reshape(256, 16),
            )
        )
    )
    out = pl.pallas_call(
        finish_kernel,
        name="finish",
        out_shape=jax.ShapeDtypeStruct((2048, 128), F32),
        in_specs=[pl.BlockSpec(memory_space=pltpu.SMEM)] + [near_by] * 6 + [held] * 2,
        out_specs=held,
        scratch_shapes=[
            vmem((2048, 128), F32),
            vmem((1024, 256), BF16),
            vmem((2048, 256), BF16),
            vmem((256, 256), BF16),
            vmem((2048, 128), F32),
            pltpu.SemaphoreType.DMA((6,)),
        ],
        compiler_params=pltpu.CompilerParams(vmem_limit_bytes=6 * 1024 * 1024),
    )(
        order,
        tiles.reshape(4096, 4, 128),
        factor_r.reshape(4096, 4, 128),
        factor_i.reshape(4096, 4, 128),
        lower,
        near,
        mask,
        pltpu.with_memory_space_constraint(parent_to_child.reshape(2048, 256), pltpu.HBM),
        pltpu.with_memory_space_constraint(receive_map, pltpu.HBM),
    )
    return out.reshape(32, 32, 2, 128)


def solution(mesh):
    in_specs = (
        P("gx", "gy", None, None),
        P("gx", "gy"),
        P(),
        P(),
        P(),
        P(),
        P("gx", "gy", None),
        P("gx", "gy", None),
        P("gx", "gy"),
        P(),
        P(),
        P(),
    )
    out_specs = P("gx", "gy", None, None)
    step = functools.partial(body, mesh.shape["gx"], mesh.shape["gy"])
    return jax.shard_map(step, mesh=mesh, in_specs=in_specs, out_specs=out_specs, check_vma=False)
```

```python
import functools

import jax
import jax.numpy as jnp
from jax import lax
from jax.experimental import pallas as pl
from jax.experimental.pallas import tpu as pltpu
from jax.sharding import PartitionSpec as P

F32 = jnp.float32
BF16 = jnp.bfloat16
MESH = pl.DeviceIdType.MESH
TX = 32
TY = 32
PITCH = 80
WIDE = TX + 4
CELLS = 256
LATER = 144
OWN = ((0, 80), (80, 64), (144, 64), (208, 48))
OTHER = OWN[2:]
OFFSETS = [(dx, dy) for dx in range(-2, 3) for dy in range(-2, 3) if max(abs(dx), abs(dy)) == 2]


def remote(src, dst, send, recv, device):
    return pltpu.make_async_remote_copy(
        src_ref=src, dst_ref=dst, send_sem=send, recv_sem=recv, device_id=device, device_id_type=MESH
    )


def gather_kernel(
    n_gx,
    n_gy,
    cur_in,
    cnt_in,
    agg_in,
    near_in,
    low_in,
    c2p_in,
    table_in,
    kind_in,
    used_in,
    list_in,
    order,
    tiles,
    factor_r,
    factor_i,
    low_v,
    near_v,
    mask_v,
    cur,
    cnt,
    agg,
    near,
    low,
    c2p,
    table,
    kind,
    used,
    source,
    group,
    tables,
    picks,
    sel_rows,
    cntb,
    lf,
    pf,
    ll,
    pv,
    own,
    s_lo,
    s_hi,
    h_lo,
    h_hi,
    ys,
    yr,
    xs,
    xr,
    hs,
    hr,
    ld,
):
    gx = lax.axis_index("gx")
    gy = lax.axis_index("gy")
    ring = n_gy // 2
    y = gy // 2
    xh = lax.rem(gy, 2)
    px = 1 - xh

    def slot(yy, xx):
        return lax.rem(yy + ring, ring) * 2 + xx

    x_next = {"gx": lax.rem(gx + 1, n_gx)}
    x_prev = {"gx": lax.rem(gx + n_gx - 1, n_gx)}
    y_next = {"gy": lax.rem(gy + 1, n_gy)}
    y_prev = {"gy": lax.rem(gy + n_gy - 1, n_gy)}
    r_next = {"gy": slot(y + 1, xh)}
    r_prev = {"gy": slot(y - 1, xh)}
    r_cross = {"gy": slot(y, px)}
    barrier = pltpu.get_barrier_semaphore()
    for device in (x_next, x_prev, y_next, y_prev, r_next, r_prev):
        pl.semaphore_signal(barrier, inc=1, device_id=device, device_id_type=MESH)

    pairs = (
        (cnt_in, cnt),
        (cur_in, cur),
        (agg_in, agg),
        (c2p_in, c2p),
        (table_in, table),
        (kind_in, kind),
        (used_in, used),
        (near_in, near),
        (low_in, low),
        (list_in, source),
    )
    loads = [pltpu.make_async_copy(src, dst, ld.at[n]) for n, (src, dst) in enumerate(pairs)]
    for copy in loads[:4]:
        copy.start()
    loads[0].wait()
    loads[1].wait()
    for copy in loads[4:]:
        copy.start()

    pick = (
        lax.broadcasted_iota(jnp.int32, (2 * TY, TY), 0) // 2 == lax.broadcasted_iota(jnp.int32, (2 * TY, TY), 1)
    ).astype(F32)
    for i in range(TX):
        line = jnp.broadcast_to(cnt[pl.ds(i, 1), :].astype(F32), (2 * TY, TY))
        sel_rows[pl.ds(2 * TY * i, 2 * TY), :] = (line * pick).astype(BF16)
    cntb[...] = jnp.dot(sel_rows[...], jnp.ones((TY, 128), BF16), preferred_element_type=F32)
    lane = lax.broadcasted_iota(jnp.int32, (2 * TY, 128), 1).astype(F32)

    def piece(ref, x, start):
        real = ref[pl.ds(PITCH * x + start, 16, stride=4), :]
        imag = ref[pl.ds(PITCH * x + start + 1, 16, stride=4), :]
        return real, imag

    def plane(x, k):
        real, imag = piece(lf, x, 6 + 2 * k)
        base = 64 * x + 16 * k
        ll[pl.ds(base, 16), :] = jnp.concatenate([real, imag], axis=1).astype(BF16)

    def lines(ref, x, count, k, planes):
        parts = [ref[pl.ds(64 * (x + n) + 16 * k, 16 * planes), :] for n in range(count)]
        return jnp.concatenate(parts, axis=0)

    def spread(x, b, value):
        for h in range(2):
            pf[pl.ds(PITCH * x + 8 + 2 * b + h, 16, stride=4), :] = value[:, 128 * h : 128 * h + 128]

    sign = (1, -1)
    along = (r_next, r_prev)
    sent = []

    def go(copy):
        copy.start()
        sent.append(copy)

    def y_copy(dr, d, w, i, mine=False):
        start, n = (OTHER if w else OWN)[i]
        where = group.at[slot(y - sign[dr] * d, px if w else xh), pl.ds(start, n)]
        k = i + len(OWN) * w
        src = own.at[pl.ds(start, n)] if mine else where
        return remote(src, where, ys.at[dr, d, k], yr.at[dr, d, k], along[dr])

    def y_arrival(dr, d, w, i):
        start, n = (OTHER if w else OWN)[i]
        where = group.at[slot(y - sign[dr] * (d + 1), px if w else xh), pl.ds(start, n)]
        k = i + len(OWN) * w
        return remote(where, where, ys.at[dr, d, k], yr.at[dr, d, k], along[dr])

    def turns(d, i):
        return (0, 1) if d < 3 else (i % 2,)

    def x_copy(j, yy, k, piece, mine=False):
        where = group.at[slot(yy, xh), pl.ds(*piece)]
        src = own.at[pl.ds(*piece)] if mine else where
        return remote(src, where, xs.at[j, k], xr.at[j, k], r_cross)

    def x_arrival(j, yy, k, piece):
        where = group.at[slot(yy, px), pl.ds(*piece)]
        return remote(where, where, xs.at[j, k], xr.at[j, k], r_cross)

    def number(d, dr):
        return 0 if d == 0 else 7 if d == 4 else 1 + 2 * (d - 1) + dr

    for part, (low_p, high_p) in enumerate(((0, LATER // 16), (LATER // 16, 16))):
        for i in range(2 * low_p, 2 * high_p):
            rows = pl.ds(2 * TY * i, 2 * TY)
            live = jnp.where(lane < cntb[rows, :], cur[rows, :].astype(F32), 0.0)
            lf[pl.ds(PITCH * (i + 2) + 8, 2 * TY), :] = live
        for i in range(2 * low_p, 2 * high_p):
            for k in (1, 2):
                plane(i + 2, k)
        if part == 0:
            loads[2].wait()
        count = high_p - low_p
        lhs = lines(ll, 2 + 2 * low_p, 2 * count, 1, 2)
        pv[pl.ds(64 * low_p, 64 * count), :] = jnp.dot(lhs, agg[...], preferred_element_type=F32).astype(BF16)
        if part == 0:
            loads[3].wait()
        total = jnp.zeros((16 * count, 512), F32)
        for q in range(4):
            child = jnp.concatenate([pv[pl.ds(64 * p + 16 * q, 16), :] for p in range(low_p, high_p)], axis=0)
            total = total + jnp.dot(child, c2p[pl.ds(256 * q, 256), :], preferred_element_type=F32)
        own[pl.ds(16 * low_p, 16 * count), :] = total.astype(BF16)
        if part == 0:
            pl.semaphore_wait(barrier, 6)
        for i in (2 * part, 2 * part + 1):
            if part == 1:
                go(x_copy(0, y, i, OWN[i], True))
            for dr in range(2):
                go(y_copy(dr, 0, 0, i, True))
            if part == 0:
                go(x_copy(0, y, i, OWN[i], True))

    def x_halo(k):
        src = (2, 3, TX, TX + 1)[k]
        dst = (TX + 2, TX + 3, 0, 1)[k]
        return remote(
            lf.at[pl.ds(PITCH * src + 8, 2 * TY)],
            lf.at[pl.ds(PITCH * dst + 8, 2 * TY)],
            hs.at[k],
            hr.at[k],
            x_prev if k < 2 else x_next,
        )

    halo = [x_halo(k) for k in range(4)]
    for copy in halo:
        copy.start()

    def unfold(sl, src, first, count):
        def line(p, _):
            rows = src[pl.ds(pl.multiple_of(16 * p, 16), 16), :].astype(F32)
            base = pl.multiple_of(1024 * p + 64 * sl, 64)
            for q in range(4):
                tiles[pl.ds(base + q, 16, stride=4), :] = rows[:, 128 * q : 128 * q + 128]
            return 0

        lax.fori_loop(first // 16, (first + count) // 16, line, 0)

    def unfold_slot(yy, xx, first, count):
        sl = slot(yy, xx)
        unfold(sl, group.at[sl], first, count)

    own_lane = lax.broadcasted_iota(jnp.int32, (16, 128), 1).astype(F32)
    for i in range(TX):
        for b in range(2):
            held = cntb[pl.ds(64 * i + 2 * b, 16, stride=4), :]
            mask_v[pl.ds(32 * i + 16 * b, 16), :] = jnp.where(own_lane < held, 1.0, 0.0)
    for i in range(TX):
        for b in range(2):
            spread(i + 2, b, pv[pl.ds(32 * i + 16 * b, 16), :].astype(F32))

    for copy in halo:
        copy.wait()

    @pl.when(gx == 0)
    def _():
        for x in (0, 1):
            lf[pl.ds(PITCH * x + 8, 2 * TY), :] = jnp.zeros((2 * TY, 128), F32)

    @pl.when(gx == n_gx - 1)
    def _():
        for x in (TX + 2, TX + 3):
            lf[pl.ds(PITCH * x + 8, 2 * TY), :] = jnp.zeros((2 * TY, 128), F32)

    for x in range(0, WIDE, 2):
        for buf, start in ((s_lo, 8), (s_hi, 2 * TY)):
            pair = [lf[pl.ds(PITCH * (x + e) + start, 8), :] for e in range(2)]
            buf[pl.ds(8 * x, 16), :] = jnp.concatenate(pair, axis=0).astype(BF16)
    halo_y = [
        remote(s_lo, h_hi, hs.at[4], hr.at[4], y_prev),
        remote(s_hi, h_lo, hs.at[5], hr.at[5], y_next),
    ]
    for copy in halo_y:
        copy.start()

    for copy in loads[4:]:
        copy.wait()
    kinds = table.shape[0] // 4
    for n in range(4):
        rest = table[pl.ds(2 * (n % 2) + n // 2, kinds, stride=4), :]
        for part in range(3):
            top = rest.astype(BF16)
            tables[pl.ds(kinds * part, kinds), pl.ds(128 * n, 128)] = top
            rest = rest - top.astype(F32)
    square = (lax.broadcasted_iota(jnp.int32, (16, 16), 0) == lax.broadcasted_iota(jnp.int32, (16, 16), 1)).astype(F32)
    spread_used = [jnp.broadcast_to(used[pl.ds(p, 1), :].astype(F32), (16, 16)) * square for p in range(16)]
    held_used = jnp.dot(
        jnp.concatenate(spread_used, axis=0).astype(BF16), jnp.ones((16, 128), BF16), preferred_element_type=F32
    )
    entry = lax.broadcasted_iota(jnp.int32, (256, 16), 1).astype(F32)
    picks[...] = jnp.where(entry < held_used[:, :16], kind[...].astype(F32), -1.0)

    group_of = lax.broadcasted_iota(jnp.int32, (32, 128), 1) // 16
    dense = jnp.zeros((32, 128), jnp.int32)
    for u in range(8):
        some = source[pl.ds(u, 32, stride=8), :]
        dense = jnp.where(group_of == u, jnp.concatenate([some] * 8, axis=1), dense)
    order[...] = dense

    def factor_part(e):
        wide = lax.rem(lax.broadcasted_iota(jnp.int32, (256, 3 * kinds), 1), kinds).astype(F32)
        choice = jnp.broadcast_to(picks[:, e : e + 1], (256, 3 * kinds)) == wide
        got = jnp.dot(jnp.where(choice, 1.0, 0.0).astype(BF16), tables[...], preferred_element_type=F32)
        for row in range(4):
            at = pl.ds(1024 * e + row, 256, stride=4)
            n = row % 2
            factor_r[at, :] = got[:, 128 * n : 128 * n + 128]
            part = got[:, 256 + 128 * n : 384 + 128 * n]
            factor_i[at, :] = -part if row >= 2 else part

    def own_step(d):
        for i in range(len(OWN)):
            for dr in turns(d - 1, i):
                y_arrival(dr, d - 1, 0, i).wait_recv()
                if i < 2:
                    go(x_copy(number(d, dr), y - sign[dr] * d, i, OWN[i]))
            if d < 4:
                for dr in turns(d, i):
                    go(y_copy(dr, d, 0, i))
        for dr in range(2 if d < 4 else 1):
            unfold_slot(y - sign[dr] * d, xh, 0, CELLS)

    def other_step(d):
        for i in range(len(OTHER)):
            if d == 0:
                x_arrival(0, y, 2 + i, OTHER[i]).wait_recv()
            else:
                for dr in turns(d - 1, i):
                    y_arrival(dr, d - 1, 1, i).wait_recv()
            if d < 4:
                for dr in turns(d, i):
                    go(y_copy(dr, d, 1, i))
        for dr in range(2 if 0 < d < 4 else 1):
            unfold_slot(y - sign[dr] * d, px, LATER, CELLS - LATER)

    def cross_step(d):
        for i in range(2):
            for dr in (0,) if d == 0 else turns(d - 1, i):
                x_arrival(number(d, dr), y - sign[dr] * d, i, OWN[i]).wait_recv()
        for dr in range(2 if 0 < d < 4 else 1):
            unfold_slot(y - sign[dr] * d, px, 0, LATER)

    unfold(gy, own, 0, CELLS)
    for e in range(4):
        factor_part(e)
    own_step(1)
    other_step(0)

    for x in (0, 1, TX + 2, TX + 3):
        for k in (1, 2):
            plane(x, k)
    for x in (0, TX + 2):
        got = jnp.dot(lines(ll, x, 2, 1, 2), agg[...], preferred_element_type=F32).astype(BF16).astype(F32)
        for e in range(2):
            for b in range(2):
                spread(x + e, b, got[32 * e + 16 * b : 32 * e + 16 * b + 16])

    for copy in halo_y:
        copy.wait()

    @pl.when(gy == 0)
    def _():
        h_lo[...] = jnp.zeros_like(h_lo)

    @pl.when(gy == n_gy - 1)
    def _():
        h_hi[...] = jnp.zeros_like(h_hi)

    for x in range(0, WIDE, 2):
        for buf, start in ((h_lo, 0), (h_hi, 2 * TY + 8)):
            pair = buf[pl.ds(8 * x, 16), :].astype(F32)
            for e in range(2):
                lf[pl.ds(PITCH * (x + e) + start, 8), :] = pair[8 * e : 8 * e + 8]

    for start in (4, 6, 2 * TY + 8, 2 * TY + 10):
        cols = [lf[pl.ds(start + h, WIDE, stride=PITCH), :] for h in range(2)]
        lhs = jnp.concatenate(cols, axis=1)
        lhs = jnp.concatenate([lhs, jnp.zeros((48 - WIDE, 256), F32)], axis=0).astype(BF16)
        got = jnp.dot(lhs, agg[...], preferred_element_type=F32).astype(BF16).astype(F32)
        for h in range(2):
            pf[pl.ds(start + h, WIDE, stride=PITCH), :] = got[:WIDE, 128 * h : 128 * h + 128]

    def near_chunk(c):
        acc = jnp.zeros((256, 256), F32)
        for dx in range(3):
            for dy in range(3):
                lhs = lines(ll, 8 * c + 1 + dx, 8, dy, 2)
                acc = acc + jnp.dot(lhs, near[pl.ds(256 * (3 * dx + dy), 256), :], preferred_element_type=F32)
        near_v[pl.ds(256 * c, 256), :] = acc

    def lower_line(i, _):
        for b in range(2):
            first = jnp.zeros((16, 128), F32)
            second = jnp.zeros((16, 128), F32)
            for k, (dx, dy) in enumerate(OFFSETS):
                base = PITCH * (i + 2 + dx) + 8 + 2 * b + 2 * dy
                real = pf[pl.ds(base, 16, stride=4), :]
                imag = pf[pl.ds(base + 1, 16, stride=4), :]
                t0 = low[pl.ds(2 * k, 1), :]
                t1 = low[pl.ds(2 * k + 1, 1), :]
                first = first + (t0 * real - t1 * imag)
                second = second + (t0 * imag + t1 * real)
            rows = pl.ds(pl.multiple_of(32 * i + 16 * b, 16), 16)
            low_v[rows, pl.ds(0, 128)] = first
            low_v[rows, pl.ds(128, 128)] = second
        return 0

    for x in range(1, WIDE - 1):
        for k in (0, 3):
            plane(x, k)
    near_chunk(0)
    near_chunk(1)
    factor_part(4)
    factor_part(5)
    own_step(2)
    other_step(1)
    cross_step(0)
    near_chunk(2)
    near_chunk(3)
    for e in range(6, 9):
        factor_part(e)
    cross_step(1)
    own_step(3)
    other_step(2)
    lax.fori_loop(0, TX // 2, lower_line, 0)
    for e in range(9, 12):
        factor_part(e)
    cross_step(2)
    settled = len(sent)
    own_step(4)
    other_step(3)
    lax.fori_loop(TX // 2, TX, lower_line, 0)
    for e in range(12, 16):
        factor_part(e)
    cross_step(3)
    for copy in sent[:settled]:
        copy.wait_send()
    other_step(4)
    cross_step(4)
    for copy in sent[settled:]:
        copy.wait_send()


def finish_kernel(order_in, tiles, factor_r, factor_i, low_v, near_v, mask_v, p2c_in, recv_in, result, sums, incoming, p2c, recv_map, out, order, sem):
    few, rest = pl.ds(0, 8), pl.ds(8, 24)
    lists = [
        pltpu.make_async_copy(order_in.at[few], order.at[few], sem.at[6]),
        pltpu.make_async_copy(order_in.at[rest], order.at[rest], sem.at[7]),
    ]
    loads = [pltpu.make_async_copy(p2c_in, p2c, sem.at[0]), pltpu.make_async_copy(recv_in, recv_map, sem.at[1])]
    for copy in lists + loads:
        copy.start()

    def targets(n, _):
        for u in range(8):
            t = 8 * n + u
            first = jnp.zeros((4, 128), F32)
            second = jnp.zeros((4, 128), F32)
            for e in range(16):
                x = tiles[order[n, 16 * u + e]]
                first = first + factor_r[t + 256 * e] * x
                second = second + factor_i[t + 256 * e] * x
            rows = pl.multiple_of(8 * t, 8)
            sums[pl.ds(rows, 4), :] = first
            sums[pl.ds(rows + 4, 4), :] = second
        return 0

    lists[0].wait()
    lax.fori_loop(0, 8, targets, 0)
    lists[1].wait()
    lax.fori_loop(8, 32, targets, 0)

    def take(row):
        return sums[pl.ds(row, 256, stride=8), :]

    parts = [take(0) + take(6), take(1) + take(7), take(2) + take(4), take(3) + take(5)]
    coarse_in = jnp.concatenate(parts, axis=1).astype(BF16)
    for copy in loads:
        copy.wait()
    for q in range(4):
        got = jnp.dot(coarse_in, p2c[pl.ds(512 * q, 512), :], preferred_element_type=F32)
        for p in range(16):
            rows = pl.ds(64 * p + 16 * q, 16)
            incoming[rows, :] = (low_v[rows, :] + got[16 * p : 16 * p + 16]).astype(BF16)
    for block in range(4):
        rows = pl.ds(256 * block, 256)
        field = jnp.dot(incoming[rows, :], recv_map[...], preferred_element_type=F32) + near_v[rows, :]
        mask = mask_v[rows, :]
        for h in range(2):
            kept = field[:, 128 * h : 128 * h + 128] * mask
            for n in range(16):
                i = 8 * block + n // 2
                out[pl.ds(64 * i + 2 * (n % 2) + h, 16, stride=4), :] = kept[16 * n : 16 * n + 16]
        done = pltpu.make_async_copy(
            out.at[pl.ds(512 * block, 512)], result.at[pl.ds(512 * block, 512)], sem.at[2 + block]
        )
        done.start()
        loads.append(done)
    for copy in loads[2:]:
        copy.wait()


def body(
    n_gx,
    n_gy,
    currents,
    box_count,
    aggregate,
    near_blocks,
    low_translator,
    child_to_parent,
    coarse_list,
    coarse_kind,
    coarse_count,
    up_translator,
    parent_to_child,
    receive_map,
):
    vmem = pltpu.VMEM
    held = pl.BlockSpec(memory_space=pltpu.HBM)
    near_by = pl.BlockSpec(memory_space=pltpu.VMEM)
    order, tiles, factor_r, factor_i, lower, near, mask = pl.pallas_call(
        functools.partial(gather_kernel, n_gx, n_gy),
        name="gather",
        out_shape=(
            jax.ShapeDtypeStruct((32, 128), jnp.int32),
            jax.ShapeDtypeStruct((16384, 128), F32),
            jax.ShapeDtypeStruct((16384, 128), F32),
            jax.ShapeDtypeStruct((16384, 128), F32),
            jax.ShapeDtypeStruct((1024, 256), F32),
            jax.ShapeDtypeStruct((1024, 256), F32),
            jax.ShapeDtypeStruct((1024, 128), F32),
        ),
        in_specs=[held] * 10,
        out_specs=(near_by,) * 7,
        scratch_shapes=[
            vmem((2048, 128), BF16),
            vmem((32, 32), jnp.int32),
            vmem((256, 256), BF16),
            vmem((2304, 256), BF16),
            vmem((32, 128), F32),
            vmem((1024, 512), BF16),
            vmem((256, 128), F32),
            vmem((256, 16), jnp.int32),
            vmem((16, 16), jnp.int32),
            vmem((256, 16), jnp.int32),
            vmem((n_gy, CELLS, 512), BF16),
            vmem((192, 512), BF16),
            vmem((256, 16), F32),
            vmem((2048, 32), BF16),
            vmem((2048, 128), F32),
            vmem((WIDE * PITCH, 128), F32),
            vmem((WIDE * PITCH, 128), F32),
            vmem((WIDE * 64, 256), BF16),
            vmem((1024, 256), BF16),
            vmem((CELLS, 512), BF16),
            vmem((WIDE * 8, 128), BF16),
            vmem((WIDE * 8, 128), BF16),
            vmem((WIDE * 8, 128), BF16),
            vmem((WIDE * 8, 128), BF16),
            pltpu.SemaphoreType.DMA((2, 4, 6)),
            pltpu.SemaphoreType.DMA((2, 4, 6)),
            pltpu.SemaphoreType.DMA((8, 4)),
            pltpu.SemaphoreType.DMA((8, 4)),
            pltpu.SemaphoreType.DMA((6,)),
            pltpu.SemaphoreType.DMA((6,)),
            pltpu.SemaphoreType.DMA((10,)),
        ],
        compiler_params=pltpu.CompilerParams(
            collective_id=0, has_side_effects=True, vmem_limit_bytes=16 * 1024 * 1024
        ),
    )(
        *(
            pltpu.with_memory_space_constraint(array, pltpu.HBM)
            for array in (
                currents.reshape(2048, 128),
                box_count,
                aggregate,
                near_blocks.reshape(2304, 256),
                low_translator.reshape(32, 128),
                child_to_parent.reshape(1024, 512),
                up_translator.reshape(64, 2, 2, 128).transpose(0, 2, 1, 3).reshape(256, 128),
                coarse_kind.reshape(256, 16),
                coarse_count,
                coarse_list.reshape(256, 16),
            )
        )
    )
    out = pl.pallas_call(
        finish_kernel,
        name="finish",
        out_shape=jax.ShapeDtypeStruct((2048, 128), F32),
        in_specs=[near_by] * 7 + [held] * 2,
        out_specs=held,
        scratch_shapes=[
            vmem((2048, 128), F32),
            vmem((1024, 256), BF16),
            vmem((2048, 256), BF16),
            vmem((256, 256), BF16),
            vmem((2048, 128), F32),
            pltpu.SMEM((32, 128), jnp.int32),
            pltpu.SemaphoreType.DMA((8,)),
        ],
        compiler_params=pltpu.CompilerParams(vmem_limit_bytes=6 * 1024 * 1024),
    )(
        order,
        tiles.reshape(4096, 4, 128),
        factor_r.reshape(4096, 4, 128),
        factor_i.reshape(4096, 4, 128),
        lower,
        near,
        mask,
        pltpu.with_memory_space_constraint(parent_to_child.reshape(2048, 256), pltpu.HBM),
        pltpu.with_memory_space_constraint(receive_map, pltpu.HBM),
    )
    return out.reshape(32, 32, 2, 128)


def solution(mesh):
    in_specs = (
        P("gx", "gy", None, None),
        P("gx", "gy"),
        P(),
        P(),
        P(),
        P(),
        P("gx", "gy", None),
        P("gx", "gy", None),
        P("gx", "gy"),
        P(),
        P(),
        P(),
    )
    out_specs = P("gx", "gy", None, None)
    step = functools.partial(body, mesh.shape["gx"], mesh.shape["gy"])
    return jax.shard_map(step, mesh=mesh, in_specs=in_specs, out_specs=out_specs, check_vma=False)
```
